32 devices in a mesh: dp: 8 (over z, x), tensor: 4 (over y, core).
Axes of the slice: x: 2, y: 2, z: 4, core: 2. Of those that a mesh axis runs over, the one named last changes fastest.
Arguments:
- tokens: bfloat16 [9344, 768], P('dp'), may hold values from -6 to 6
- cotangent: bfloat16 [9344, 768], P('dp'), may hold values from -6 to 6
- image_group: int32 [16], replicated, may hold values from 0 to 7, as said below
- image_length: int32 [16], replicated, may hold values from 197 to 577, as said below
- first_gain: float32 [768], replicated, may hold values from 0.5 to 1.5
- first_shift: float32 [768], replicated, may hold values from -1.25 to 1.25
- qkv_weight: bfloat16 [768, 3, 768], P(None, None, 'tensor'), may hold values from -0.21875 to 0.21875
- qv_bias: float32 [2, 768], P(None, 'tensor'), may hold values from -3 to 3
- out_weight: bfloat16 [768, 768], P('tensor'), may hold values from -1.5 to 1.5
- out_bias: float32 [768], replicated, may hold values from -1.75 to 1.75
- second_gain: float32 [768], replicated, may hold values from 0.5 to 1.5
- second_shift: float32 [768], replicated, may hold values from -1.25 to 1.25
- up_weight: bfloat16 [768, 3072], P(None, 'tensor'), may hold values from -0.21875 to 0.21875
- up_bias: float32 [3072], P('tensor'), may hold values from -3 to 3
- down_weight: bfloat16 [3072, 768], P('tensor'), may hold values from -0.109375 to 0.109375
- down_bias: float32 [768], replicated, may hold values from -1.75 to 1.75
Outputs:
- block_out: bfloat16 [9344, 768], P('dp')
- input_grad: float32 [9344, 768], P('dp')
- first_gain_grad: float32 [768], replicated
- first_shift_grad: float32 [768], replicated
- qkv_weight_grad: float32 [768, 3, 768], P(None, None, 'tensor')
- qv_bias_grad: float32 [2, 768], P(None, 'tensor')
- out_weight_grad: float32 [768, 768], P('tensor')
- out_bias_grad: float32 [768], replicated
- second_gain_grad: float32 [768], replicated
- second_shift_grad: float32 [768], replicated
- up_weight_grad: float32 [768, 3072], P(None, 'tensor')
- up_bias_grad: float32 [3072], P('tensor')
- down_weight_grad: float32 [3072, 768], P('tensor')
- down_bias_grad: float32 [768], replicated
The draws below stay inside these ranges and needn't reach their ends.
Inputs may be any that keep to these rules, and one draw needn't show every extreme that they name: `image_group`: exactly 2 images name each data group. `image_length`: every entry is 197 or 577; in every draw some data group holds 2 images of 577 tokens and another only images of 197 tokens.
All inputs are finite; a program needn't handle non-finite values.
Results may differ from the reference program's by a relative error of at most 0.018.
Values may be sent and summed in bfloat16 or wider, within the bound.
A program may use at most 128 MiB of HBM per device.

```python
import jax
import jax.numpy as jnp
from jax import lax

D = 768
HD = 64
FF = 3072
RES_SMALL = 197
RES_LARGE = 577
IMG_GRP = 2
TOK_DEV = 1168
IMAGES = 16
TOKENS = 9344
N_DP = 8
N_TENSOR = 4


def draw_image_group(key, part):
    order = jax.random.permutation(jax.random.fold_in(key, 11), IMAGES)
    return (order // IMG_GRP).astype(jnp.int32)


def draw_image_length(key, part):
    groups = draw_image_group(key, part)
    group_total = IMAGES // IMG_GRP
    picks = jax.random.randint(jax.random.fold_in(key, 12), (IMAGES,), 0, 20)
    lengths = jnp.where(picks < 7, RES_LARGE, RES_SMALL)
    chosen = jax.random.randint(jax.random.fold_in(key, 13), (), 0, group_total)
    lengths = jnp.where(groups == chosen, RES_LARGE, lengths)
    lengths = jnp.where(groups == (chosen + 1) % group_total, RES_SMALL, lengths)
    return lengths.astype(jnp.int32)


def block_levels(rng, extent, pieces, smallest, high):
    def one(dim, blocks):
        draws = jax.random.uniform(jax.random.fold_in(jax.random.fold_in(rng, 6), dim), (blocks,), jnp.float32, smallest / len(pieces), high / len(pieces))
        return jnp.repeat(jnp.exp(draws), extent[dim] // blocks).reshape((-1,) + (1,) * (len(extent) - dim - 1))

    factor_of = one(*pieces[0])
    for cut in pieces[1:]:
        factor_of = factor_of * one(*cut)
    return factor_of


def scatter_about(key, extent, width, limit, shards=(), kind=jnp.bfloat16):
    drawn = width * jax.random.normal(key, extent, jnp.float32)
    if shards:
        drawn = drawn * block_levels(key, extent, shards, -0.22, 0.18)
    return jnp.clip(drawn, -limit, limit).astype(kind)


def setup_inputs(seed: int = 0) -> dict:
    key_list = jax.random.split(jax.random.key(seed), 17)
    tokens = scatter_about(key_list[0], (TOKENS, D), 1.0, 6.0, ((0, 8),))
    cotangent = scatter_about(key_list[1], (TOKENS, D), 1.0, 6.0, ((0, 8),))
    image_group = draw_image_group(jax.random.fold_in(key_list[16], 71), 0)
    image_length = draw_image_length(jax.random.fold_in(key_list[16], 71), 0)
    first_gain = jnp.clip(1.0 + 0.1 * jax.random.normal(key_list[4], (D,), jnp.float32), 0.5, 1.5)
    first_shift = scatter_about(key_list[5], (D,), 0.2, 1.25, (), jnp.float32)
    qkv_weight = scatter_about(key_list[6], (D, 3, D), D ** -0.5, 0.21875, ((2, 4),))
    qv_bias = scatter_about(key_list[7], (2, D), 0.5, 3.0, ((1, 4),), jnp.float32)
    out_weight = scatter_about(key_list[8], (D, D), 16 ** -0.5, 1.5, ((0, 4),))
    out_bias = scatter_about(key_list[9], (D,), 0.3, 1.75, (), jnp.float32)
    second_gain = jnp.clip(1.0 + 0.1 * jax.random.normal(key_list[10], (D,), jnp.float32), 0.5, 1.5)
    second_shift = scatter_about(key_list[11], (D,), 0.2, 1.25, (), jnp.float32)
    up_weight = scatter_about(key_list[12], (D, FF), D ** -0.5, 0.21875, ((1, 4),))
    up_bias = scatter_about(key_list[13], (FF,), 0.5, 3.0, ((0, 4),), jnp.float32)
    down_weight = scatter_about(key_list[14], (FF, D), FF ** -0.5, 0.109375, ((0, 4),))
    down_bias = scatter_about(key_list[15], (D,), 0.3, 1.75, (), jnp.float32)
    return {"tokens": tokens, "cotangent": cotangent, "image_group": image_group, "image_length": image_length, "first_gain": first_gain, "first_shift": first_shift, "qkv_weight": qkv_weight, "qv_bias": qv_bias, "out_weight": out_weight, "out_bias": out_bias, "second_gain": second_gain, "second_shift": second_shift, "up_weight": up_weight, "up_bias": up_bias, "down_weight": down_weight, "down_bias": down_bias}


EPSILON = 1e-06
MASKED = -1e+30
HIGH = lax.Precision.HIGHEST

@jax.custom_vjp
def low(v):
    return lax.optimization_barrier(v.astype(jnp.bfloat16)).astype(jnp.float32)

@jax.custom_vjp
def low_back(v):
    return v

def low_keep(v):
    return (low(v), None)

def low_pass(kept, grad):
    return (grad,)

def back_keep(v):
    return (v, None)

def back_low(kept, grad):
    return (low(grad),)
low.defvjp(low_keep, low_pass)
low_back.defvjp(back_keep, back_low)

def layer_norm(token_rows, gain_row, shift_row):
    average = lax.optimization_barrier(jnp.mean(token_rows, axis=-1, keepdims=True))
    centered = token_rows - average
    variance = lax.optimization_barrier(jnp.mean(centered * centered, axis=-1, keepdims=True))
    return centered * lax.rsqrt(variance + EPSILON) * gain_row + shift_row

def segment_rows(image_group, image_length, group_index, row_count):
    in_group = image_group == group_index
    lengths = jnp.where(in_group, image_length, 0).astype(jnp.int32)
    run_ends = jnp.cumsum(lengths).astype(jnp.int32)
    position = jnp.arange(row_count, dtype=jnp.int32)
    finished = (position[:, None] >= run_ends[None, :]) & in_group[None, :]
    segment = lax.optimization_barrier(jnp.sum(finished.astype(jnp.int32), axis=1)).astype(jnp.int32)
    return (segment, position < run_ends[-1])

def group_forward(parameters, token_rows, segment):
    first_gain, first_shift, qkv_weight, qv_bias, out_weight, out_bias, second_gain, second_shift, up_weight, up_bias, down_weight, down_bias = parameters
    row_count, model_width = token_rows.shape
    shard_width = model_width // N_TENSOR
    heads_part = shard_width // HD
    hidden_part = up_weight.shape[1] // N_TENSOR
    normed = low(layer_norm(token_rows, first_gain, first_shift))
    copies = low_back(jnp.broadcast_to(normed, (N_TENSOR, row_count, model_width)))
    projected = jnp.einsum('ard,dsac->sarc', copies, qkv_weight.reshape(model_width, 3, N_TENSOR, shard_width), precision=HIGH)
    bias_parts = qv_bias.reshape(2, N_TENSOR, 1, shard_width)
    queries = low_back(low(projected[0] + bias_parts[0]))
    key_rows = low_back(low(projected[1]))
    value_rows = low_back(low(projected[2] + bias_parts[1]))
    head_shape = (N_TENSOR, row_count, heads_part, HD)
    scores = jnp.einsum('aqhe,akhe->ahqk', queries.reshape(head_shape), key_rows.reshape(head_shape), precision=HIGH) * HD ** (-0.5)
    scores = low_back(scores)
    same_image = segment[:, None] == segment[None, :]
    scores = jnp.where(same_image[None, None], scores, MASKED)
    weights = low(jax.nn.softmax(scores, axis=-1))
    attended = jnp.einsum('ahqk,akhe->aqhe', weights, value_rows.reshape(head_shape), precision=HIGH)
    attended = low_back(low(attended.reshape(N_TENSOR, row_count, shard_width)))
    partial_attn = jnp.einsum('aqc,acd->aqd', attended, out_weight.reshape(N_TENSOR, shard_width, model_width), precision=HIGH)
    middle = token_rows + lax.optimization_barrier(jnp.sum(low_back(low(partial_attn)), axis=0)) + out_bias
    normed_two = low(layer_norm(middle, second_gain, second_shift))
    copies_two = low_back(jnp.broadcast_to(normed_two, (N_TENSOR, row_count, model_width)))
    pre = jnp.einsum('ard,daf->arf', copies_two, up_weight.reshape(model_width, N_TENSOR, hidden_part), precision=HIGH) + up_bias.reshape(N_TENSOR, 1, hidden_part)
    hidden = low(jax.nn.gelu(low_back(pre), approximate=False))
    partial_mlp = jnp.einsum('arf,afd->ard', hidden, down_weight.reshape(N_TENSOR, hidden_part, model_width), precision=HIGH)
    return middle + lax.optimization_barrier(jnp.sum(low_back(low(partial_mlp)), axis=0)) + down_bias

def reference(tokens, cotangent, image_group, image_length, first_gain, first_shift, qkv_weight, qv_bias, out_weight, out_bias, second_gain, second_shift, up_weight, up_bias, down_weight, down_bias):
    model_width = tokens.shape[1]
    parameters = tuple((argument.astype(jnp.float32) for argument in (first_gain, first_shift, qkv_weight, qv_bias, out_weight, out_bias, second_gain, second_shift, up_weight, up_bias, down_weight, down_bias)))
    group_ids = jnp.arange(N_DP, dtype=jnp.int32)
    segments, valid_rows = jax.vmap(lambda group_index: segment_rows(image_group, image_length, group_index, TOK_DEV))(group_ids)
    token_rows = tokens.astype(jnp.float32).reshape(N_DP, TOK_DEV, model_width)

    def forward_all(parameters, token_rows):
        single = jax.checkpoint(lambda block_item: group_forward(parameters, block_item[0], block_item[1]))
        return lax.map(single, (token_rows, segments))
    outputs, pullback = jax.vjp(forward_all, parameters, token_rows)
    keep_rows = valid_rows.astype(jnp.float32)[..., None]
    block_out = (outputs * keep_rows).astype(jnp.bfloat16).reshape(tokens.shape)
    param_grads, row_grads = pullback(cotangent.astype(jnp.float32).reshape(token_rows.shape) * keep_rows)
    first_gain_grad, first_shift_grad, qkv_weight_grad, qv_bias_grad, out_weight_grad, out_bias_grad, second_gain_grad, second_shift_grad, up_weight_grad, up_bias_grad, down_weight_grad, down_bias_grad = param_grads
    input_grad = row_grads.reshape(tokens.shape)
    return (block_out, input_grad, first_gain_grad, first_shift_grad, qkv_weight_grad, qv_bias_grad, out_weight_grad, out_bias_grad, second_gain_grad, second_shift_grad, up_weight_grad, up_bias_grad, down_weight_grad, down_bias_grad)
```

```python
import functools

import jax
import jax.numpy as jnp
from jax import lax
from jax.experimental import pallas as pl
from jax.experimental.pallas import tpu as pltpu
from jax.sharding import PartitionSpec as P

HD = 64
RES_SMALL = 197
RES_LARGE = 577
SLOT = 608
HALF = 304
EPS = 1e-06
MASKED = -1e30
BF = jnp.bfloat16
F32 = jnp.float32
MESH = pl.DeviceIdType.MESH


def dot_nn(a, b):
    return lax.dot_general(a, b, (((1,), (0,)), ((), ())), preferred_element_type=F32)


def dot_nt(a, b):
    return lax.dot_general(a, b, (((1,), (1,)), ((), ())), preferred_element_type=F32)


def dot_tn(a, b):
    return lax.dot_general(a, b, (((0,), (0,)), ((), ())), preferred_element_type=F32)


def normalize(x):
    mean = jnp.mean(x, axis=-1, keepdims=True)
    centered = x - mean
    var = jnp.mean(centered * centered, axis=-1, keepdims=True)
    scale = lax.rsqrt(var + EPS)
    return centered * scale, scale


def norm_back(u, xn, scale):
    return scale * (
        u
        - jnp.mean(u, axis=-1, keepdims=True)
        - xn * jnp.mean(u * xn, axis=-1, keepdims=True)
    )


def fold8(x):
    return jnp.sum(x.reshape(x.shape[0] // 8, 8, x.shape[1]), axis=0)


def flip(index, stride):
    return index + stride - 2 * stride * ((index // stride) % 2)


def layer_kernel(
    n_dp,
    lens,
    tok,
    cot,
    wqkv,
    wout,
    wup,
    wdown,
    g1,
    b1,
    ob,
    g2,
    b2,
    db,
    ub,
    qvb,
    block_o,
    ingrad_o,
    grads_o,
    small_o,
    normed,
    qkv,
    att,
    probs,
    normed2,
    hidden,
    pregrad,
    middle,
    midgrad,
    mg,
    agrad,
    dqkv,
    dacc,
    tmp_a,
    tmp_b,
    acc,
    accv,
    csend,
    crecv,
    ysend,
    yrecv,
    gbuf,
    rs0,
    rs1,
    rs2,
    rx,
    smc,
    smr,
    c_send,
    c_recv,
    y_send,
    y_recv,
    g_send,
    g_recv,
    d_send,
    d_recv,
    s_send,
    s_recv,
):
    levels = n_dp.bit_length() - 1
    scat = min(3, levels)
    d = lax.axis_index("dp")
    t = lax.axis_index("tensor")
    core = t % 2
    core_peer = (d, flip(t, 1))
    y_peer = (d, flip(t, 2))

    def dp_peer(level):
        return (flip(d, 2**level), t)

    bar = pltpu.get_barrier_semaphore()
    peers = [core_peer, y_peer] + [dp_peer(i) for i in range(levels)]
    for peer in peers:
        pl.semaphore_signal(bar, inc=1, device_id=peer, device_id_type=MESH)
    pl.semaphore_wait(bar, len(peers))

    own = pl.multiple_of(core * HALF, 16)
    other = pl.multiple_of((1 - core) * HALF, 16)
    width = tok.shape[1]
    heads = wout.shape[0] // HD
    rows16 = HALF // 16
    lane_head = lax.broadcasted_iota(jnp.int32, (1, wout.shape[0]), 1) // HD

    def slot_rows(s, off, size):
        return pl.ds(pl.multiple_of(s * SLOT + off, 16), size)

    def remote(src, dst, send, recv, peer):
        return pltpu.make_async_remote_copy(
            src_ref=src, dst_ref=dst, send_sem=send, recv_sem=recv, device_id=peer, device_id_type=MESH
        )

    def c_copy(s, k):
        return remote(csend, crecv.at[s, k], c_send.at[s, k], c_recv.at[s, k], core_peer)

    def y_copy(s, k):
        return remote(ysend.at[s, k], yrecv.at[s, k], y_send.at[s, k], y_recv.at[s, k], y_peer)

    def gather_copy(ref, s, k):
        region = slot_rows(s, own, HALF)
        return remote(ref.at[region], ref.at[region], g_send.at[s, k], g_recv.at[s, k], core_peer)

    def stage(s, k, part):
        csend[...] = part(other).astype(BF)
        copy = c_copy(s, k)
        copy.start()
        tmp_a[...] = part(own)
        copy.wait()

        def add(i, carry):
            r = pl.ds(pl.multiple_of(i * 16, 16), 16)
            ysend[s, k, r, :] = (tmp_a[r, :] + crecv[s, k, r, :].astype(F32)).astype(BF)
            return carry

        lax.fori_loop(0, rows16, add, 0)
        y_copy(s, k).start()

    def total(s, k, r):
        return ysend[s, k, r, :].astype(F32) + yrecv[s, k, r, :].astype(F32)

    step = [768 >> (i + 1) for i in range(scat)]

    def bit(level):
        return (d // 2**level) % 2

    def base(level):
        off = 0
        for i in range(level):
            off = off + bit(i) * step[i]
        return off

    rs = [rs0, rs1, rs2]

    def dp_rs(p, i):
        src = pl.ds(pl.multiple_of(base(i) + (1 - bit(i)) * step[i], 16), step[i])
        return remote(gbuf.at[p, src], rs[i].at[p], d_send.at[p, i], d_recv.at[p, i], dp_peer(i))

    def dp_add(p, i):
        dp_rs(p, i).wait()
        off = base(i) + bit(i) * step[i]
        out = grads_o if i == scat - 1 else gbuf

        def add(j, carry):
            r = pl.ds(pl.multiple_of(off + j * 32, 16), 32)
            rr = pl.ds(pl.multiple_of(j * 32, 16), 32)
            out[p, r, :] = (gbuf[p, r, :].astype(F32) + rs[i][p, rr, :].astype(F32)).astype(BF)
            return carry

        lax.fori_loop(0, step[i] // 32, add, 0)
        if i + 1 < scat:
            dp_rs(p, i + 1).start()

    def dp_extra(p):
        size = step[scat - 1]
        mine = pl.ds(pl.multiple_of(base(scat), 16), size)
        for e in range(levels - scat):
            copy = remote(
                grads_o.at[p, mine], rx.at[e, p], d_send.at[p, 6 + e], d_recv.at[p, 6 + e], dp_peer(scat + e)
            )
            copy.start()
            copy.wait()
            grads_o[p, mine, :] = (grads_o[p, mine, :].astype(F32) + rx[e, p].astype(F32)).astype(BF)

    def dp_ag(p, i):
        region = pl.ds(pl.multiple_of(base(i + 1), 16), step[i])
        return remote(
            grads_o.at[p, region], grads_o.at[p, region], d_send.at[p, 3 + i], d_recv.at[p, 3 + i], dp_peer(i)
        )

    def dp_last(p):
        dp_add(p, scat - 1)
        dp_extra(p)
        dp_ag(p, scat - 1).start()

    def dp_gather(p, i):
        dp_ag(p, i).wait()
        if i > 0:
            dp_ag(p, i - 1).start()

    acc[...] = jnp.zeros_like(acc)
    accv[...] = jnp.zeros_like(accv)

    def forward_attention(s, carry):
        def norm_rows(i, carry):
            r = slot_rows(s, i * 32, 32)
            xn, _ = normalize(tok[r, :].astype(F32))
            normed[r, :] = (xn * g1[...] + b1[...]).astype(BF)
            return carry

        lax.fori_loop(0, SLOT // 32, norm_rows, 0)

        def project(i, carry):
            r = slot_rows(s, i * HALF, HALF)
            x = normed[r, :]
            qkv[0, r, :] = (dot_nn(x, wqkv[0]) + qvb[0:1, :]).astype(BF)
            qkv[1, r, :] = dot_nn(x, wqkv[1]).astype(BF)
            qkv[2, r, :] = (dot_nn(x, wqkv[2]) + qvb[1:2, :]).astype(BF)
            return carry

        lax.fori_loop(0, 2, project, 0)
        whole = slot_rows(s, 0, SLOT)
        length = jnp.where(s == 0, lens[0], lens[1])
        key_bias = jnp.where(lax.broadcasted_iota(jnp.int32, (1, SLOT), 1) < length, 0.0, MASKED)

        def attend(i, carry):
            r = slot_rows(s, i * HALF, HALF)
            for h in range(heads):
                q = jnp.where(lane_head == h, qkv[0, r, :] * HD**-0.5, 0.0).astype(BF)
                scores = dot_nt(q, qkv[1, whole, :]) + key_bias
                exps = jnp.exp(scores - jnp.max(scores, axis=-1, keepdims=True))
                weights = (exps * (1.0 / jnp.sum(exps, axis=-1, keepdims=True))).astype(BF)
                probs[s * heads + h, pl.ds(pl.multiple_of(i * HALF, 16), HALF), :] = weights
                part = dot_nn(weights, qkv[2, whole, :])
                result = part if h == 0 else jnp.where(lane_head == h, part, result)
            att[r, :] = result.astype(BF)
            return carry

        lax.fori_loop(0, 2, attend, 0)
        stage(s, 0, lambda off: dot_nn(att[slot_rows(s, off, HALF), :], wout[...]))
        return carry

    lax.fori_loop(0, 2, forward_attention, 0)

    def second_norm(s):
        y_copy(s, 0).wait()

        def rows(i, carry):
            r = pl.ds(pl.multiple_of(i * 16, 16), 16)
            g = slot_rows(s, own + i * 16, 16)
            m = total(s, 0, r) + tok[g, :].astype(F32) + ob[...]
            middle[s, r, :] = m
            xn, _ = normalize(m)
            normed2[g, :] = (xn * g2[...] + b2[...]).astype(BF)
            return carry

        lax.fori_loop(0, rows16, rows, 0)
        gather_copy(normed2, s, 0).start()

    def feed_forward(s, carry):
        second_norm(s)
        gather_copy(normed2, s, 0).wait()

        def half(i, carry):
            r = slot_rows(s, i * HALF, HALF)
            tmp_a[...] = dot_nn(normed2[r, :], wup[...])
            tmp_b[...] = dot_nt(cot[r, :], wdown[...])

            def rows(j, sums):
                rr = pl.ds(pl.multiple_of(j * 16, 16), 16)
                g = slot_rows(s, i * HALF + j * 16, 16)
                x = tmp_a[rr, :] + ub[...]
                phi = 0.5 + 0.5 * lax.erf(x * 0.7071067811865476)
                hidden[g, :] = (x * phi).astype(BF)
                slope = phi + x * (jnp.exp(x * x * -0.5) * 0.3989422804014327)
                low = (tmp_b[rr, :] * slope).astype(BF)
                pregrad[g, :] = low
                return sums + fold8(low.astype(F32))

            acc[6] += lax.fori_loop(0, rows16, rows, jnp.zeros((8, width), F32))
            return carry

        lax.fori_loop(0, 2, half, 0)
        stage(s, 1, lambda off: dot_nt(pregrad[slot_rows(s, off, HALF), :], wup[...]))
        return carry

    lax.fori_loop(0, 2, feed_forward, 0)

    def weight_grad(p, left, right):
        size = step[0] if scat else 768
        for mine in (0, 1):
            off = pl.multiple_of((bit(0) if mine else 1 - bit(0)) * size, 128)
            for part in range(2):
                o = pl.multiple_of(off + part * (size // 2), 64)
                gbuf[p, pl.ds(o, size // 2), :] = dot_tn(
                    left[:, pl.ds(pl.multiple_of(off, 128), size)][:, part * (size // 2) : (part + 1) * (size // 2)],
                    right[...],
                ).astype(BF)
            if not mine:
                dp_rs(p, 0).start()

    weight_grad(0, hidden, cot)
    weight_grad(1, normed2, pregrad)

    def feed_forward_out(s, carry):
        stage(s, 2, lambda off: dot_nn(hidden[slot_rows(s, off, HALF), :], wdown[...]))
        return carry

    lax.fori_loop(0, 2, feed_forward_out, 0)

    def second_back(s):
        y_copy(s, 1).wait()

        def rows(i, sums):
            r = pl.ds(pl.multiple_of(i * 16, 16), 16)
            g = slot_rows(s, own + i * 16, 16)
            n = total(s, 1, r)
            xn, scale = normalize(middle[s, r, :])
            og = cot[g, :].astype(F32)
            m = og + norm_back(n * g2[...], xn, scale)
            midgrad[s, r, :] = m
            mg[g, :] = m.astype(BF)
            return tuple(a + fold8(b) for a, b in zip(sums, (n * xn, n, m, og), strict=True))

        zero = jnp.zeros((8, width), F32)
        sums = lax.fori_loop(0, rows16, rows, (zero,) * 4)
        for i in range(4):
            acc[2 + i] += sums[i]
        gather_copy(mg, s, 1).start()

    def attention_back(s, services):
        second_back(s)
        services[0]()
        gather_copy(mg, s, 1).wait()
        whole = slot_rows(s, 0, SLOT)
        agrad[whole, :] = dot_nt(mg[whole, :], wout[...]).astype(BF)
        dacc[...] = jnp.zeros_like(dacc)

        def chunk(i, carry):
            r = slot_rows(s, i * HALF, HALF)
            for h in range(heads):
                mask = lane_head == h
                do = agrad[r, :]
                w = probs[s * heads + h, pl.ds(pl.multiple_of(i * HALF, 16), HALF), :]
                prob_grad = dot_nt(jnp.where(mask, do, 0.0).astype(BF), qkv[2, whole, :])
                p = w.astype(F32)
                inner = jnp.sum(p * prob_grad, axis=-1, keepdims=True)
                score_grad = (p * (prob_grad - inner)).astype(BF)
                part = dot_nn(score_grad, qkv[1, whole, :])
                dq = part if h == 0 else jnp.where(mask, part, dq)
                dacc[0] += jnp.where(mask, dot_tn(score_grad, qkv[0, r, :]), 0.0)
                dacc[1] += jnp.where(mask, dot_tn(w, do), 0.0)
            low = (dq * HD**-0.5).astype(BF)
            dqkv[0, r, :] = low
            accv[0] += fold8(low.astype(F32))
            return carry

        lax.fori_loop(0, 2, chunk, 0)
        services[1]()
        dqkv[1, whole, :] = (dacc[0] * HD**-0.5).astype(BF)
        low = dacc[1].astype(BF)
        dqkv[2, whole, :] = low
        accv[1] += fold8(low.astype(F32))

        def part(off):
            r = slot_rows(s, off, HALF)
            return (
                dot_nt(dqkv[0, r, :], wqkv[0]) + dot_nt(dqkv[1, r, :], wqkv[1]) + dot_nt(dqkv[2, r, :], wqkv[2])
            )

        stage(s, 3, part)
        services[2]()

    def serve(*calls):
        def run():
            for f, p, i in calls:
                f(p, i)

        return run

    nothing = serve()
    full = scat == 3
    attention_back(0, (nothing, serve((dp_add, 0, 0)) if full else nothing, nothing))
    attention_back(
        1,
        (
            serve((dp_add, 1, 0)) if full else nothing,
            serve((dp_add, 0, 1)) if full else nothing,
            nothing,
        ),
    )

    third = wout.shape[0]
    gbuf[2, 0:third, :] = dot_tn(att[...], mg[...]).astype(BF)
    for j in range(3):
        gbuf[2, (j + 1) * third : (j + 2) * third, :] = dot_tn(dqkv[j], normed[...]).astype(BF)
    if scat:
        dp_rs(2, 0).start()

    def finish(s, carry):
        y_copy(s, 2).wait()

        def out_rows(i, carry):
            r = pl.ds(pl.multiple_of(i * 16, 16), 16)
            g = slot_rows(s, own + i * 16, 16)
            block_o[g, :] = (middle[s, r, :] + total(s, 2, r) + db[...]).astype(BF)
            return carry

        lax.fori_loop(0, rows16, out_rows, 0)
        gather_copy(block_o, s, 2).start()
        y_copy(s, 3).wait()

        def rows(i, sums):
            r = pl.ds(pl.multiple_of(i * 16, 16), 16)
            g = slot_rows(s, own + i * 16, 16)
            n = total(s, 3, r)
            xn, scale = normalize(tok[g, :].astype(F32))
            ingrad_o[g, :] = (midgrad[s, r, :] + norm_back(n * g1[...], xn, scale)).astype(BF)
            return tuple(a + fold8(b) for a, b in zip(sums, (n * xn, n), strict=True))

        zero = jnp.zeros((8, width), F32)
        sums = lax.fori_loop(0, rows16, rows, (zero,) * 2)
        for i in range(2):
            acc[i] += sums[i]
        gather_copy(ingrad_o, s, 3).start()
        return carry

    lax.fori_loop(0, 2, finish, 0)

    for i in range(7):
        row = i if i < 6 else 8
        small_o[row : row + 1, :] = jnp.sum(acc[i], axis=0, keepdims=True)
    small_o[6:8, :] = jnp.zeros((2, width), F32)
    small_o[9:16, :] = jnp.zeros((7, width), F32)
    for i in range(2):
        small_o[9 + i : 10 + i, 0:third] = jnp.sum(accv[i], axis=0, keepdims=True)
    copy = remote(small_o.at[0:8], smc, s_send.at[0], s_recv.at[0], core_peer)
    copy.start()
    copy.wait()
    small_o[0:8, :] = small_o[0:8, :] + smc[...]
    for i in range(levels):
        copy = remote(small_o, smr.at[i], s_send.at[1 + i], s_recv.at[1 + i], dp_peer(i))
        copy.start()
        copy.wait()
        small_o[...] = small_o[...] + smr[i]

    def drain(s, carry):
        gather_copy(block_o, s, 2).wait()
        gather_copy(ingrad_o, s, 3).wait()
        return carry

    lax.fori_loop(0, 2, drain, 0)

    dp_add(1, 1)
    dp_last(0)
    dp_add(2, 0)
    dp_last(1)
    dp_gather(0, 2)
    dp_add(2, 1)
    dp_gather(1, 2)
    dp_gather(0, 1)
    dp_last(2)
    dp_gather(1, 1)
    dp_gather(0, 0)
    dp_gather(2, 2)
    dp_gather(1, 0)
    dp_gather(2, 1)
    dp_gather(2, 0)


def call_layer(n_dp, *operands):
    tok = operands[1]
    rows, width = tok.shape
    third = operands[4].shape[0]
    heads = third // HD
    levels = n_dp.bit_length() - 1
    extra = max(levels - 3, 1)
    vmem = pl.BlockSpec(memory_space=pltpu.VMEM)
    dma = pltpu.SemaphoreType.DMA
    return pl.pallas_call(
        functools.partial(layer_kernel, n_dp),
        out_shape=(
            jax.ShapeDtypeStruct((rows, width), BF),
            jax.ShapeDtypeStruct((rows, width), BF),
            jax.ShapeDtypeStruct((3, width, width), BF),
            jax.ShapeDtypeStruct((16, width), F32),
        ),
        in_specs=[pl.BlockSpec(memory_space=pltpu.SMEM)] + [vmem] * (len(operands) - 1),
        out_specs=(vmem,) * 4,
        scratch_shapes=[
            pltpu.VMEM((rows, width), BF),
            pltpu.VMEM((3, rows, third), BF),
            pltpu.VMEM((rows, third), BF),
            pltpu.VMEM((2 * heads, SLOT, SLOT), BF),
            pltpu.VMEM((rows, width), BF),
            pltpu.VMEM((rows, width), BF),
            pltpu.VMEM((rows, width), BF),
            pltpu.VMEM((2, HALF, width), F32),
            pltpu.VMEM((2, HALF, width), F32),
            pltpu.VMEM((rows, width), BF),
            pltpu.VMEM((rows, third), BF),
            pltpu.VMEM((3, rows, third), BF),
            pltpu.VMEM((2, SLOT, third), F32),
            pltpu.VMEM((HALF, width), F32),
            pltpu.VMEM((HALF, width), F32),
            pltpu.VMEM((7, 8, width), F32),
            pltpu.VMEM((2, 8, third), F32),
            pltpu.VMEM((HALF, width), BF),
            pltpu.VMEM((2, 4, HALF, width), BF),
            pltpu.VMEM((2, 4, HALF, width), BF),
            pltpu.VMEM((2, 4, HALF, width), BF),
            pltpu.VMEM((3, width, width), BF),
            pltpu.VMEM((3, width // 2, width), BF),
            pltpu.VMEM((3, width // 4, width), BF),
            pltpu.VMEM((3, width // 8, width), BF),
            pltpu.VMEM((extra, 3, width // 8, width), BF),
            pltpu.VMEM((8, width), F32),
            pltpu.VMEM((levels, 16, width), F32),
            dma((2, 4)),
            dma((2, 4)),
            dma((2, 4)),
            dma((2, 4)),
            dma((2, 4)),
            dma((2, 4)),
            dma((3, 6 + extra)),
            dma((3, 6 + extra)),
            dma((1 + levels,)),
            dma((1 + levels,)),
        ],
        compiler_params=pltpu.CompilerParams(
            collective_id=0, has_side_effects=True, vmem_limit_bytes=67043328
        ),
    )(*operands)


def group_lengths(image_group, image_length, group):
    in_group = image_group == group
    number = jnp.arange(image_group.shape[0], dtype=jnp.int32)
    first = jnp.min(jnp.where(in_group, number, image_group.shape[0]))
    length0 = jnp.sum(jnp.where(number == first, image_length, 0))
    return length0, jnp.sum(jnp.where(in_group, image_length, 0)) - length0


def to_slots(rows, length0, length1):
    row = jnp.arange(SLOT, dtype=jnp.int32)[:, None]
    small = rows[RES_SMALL : RES_SMALL + SLOT]
    large = jnp.pad(rows[RES_LARGE:], ((0, RES_LARGE + SLOT - rows.shape[0]), (0, 0)))
    zero = jnp.zeros((), rows.dtype)
    one = jnp.where(row < length0, rows[:SLOT], zero)
    two = jnp.where(row < length1, jnp.where(length0 == RES_SMALL, small, large), zero)
    return jnp.concatenate([one, two], axis=0)


def from_slots(slots, row_count, length0, length1):
    row = jnp.arange(row_count, dtype=jnp.int32)[:, None]
    small = jnp.concatenate([slots[:RES_SMALL], jnp.pad(slots[SLOT:], ((0, row_count - RES_SMALL - SLOT), (0, 0)))])
    large = jnp.concatenate([slots[:RES_LARGE], slots[SLOT : SLOT + row_count - RES_LARGE]])
    return jnp.where(row < length0 + length1, jnp.where(length0 == RES_SMALL, small, large), jnp.zeros((), slots.dtype))


def body(
    n_dp,
    tokens,
    cotangent,
    image_group,
    image_length,
    first_gain,
    first_shift,
    qkv_weight,
    qv_bias,
    out_weight,
    out_bias,
    second_gain,
    second_shift,
    up_weight,
    up_bias,
    down_weight,
    down_bias,
):
    third = out_weight.shape[0]
    width = tokens.shape[1]
    length0, length1 = group_lengths(image_group, image_length, lax.axis_index("dp"))
    block, ingrad, grads, small = call_layer(
        n_dp,
        jnp.stack([length0, length1]),
        to_slots(tokens, length0, length1),
        to_slots(cotangent, length0, length1),
        jnp.transpose(qkv_weight, (1, 0, 2)),
        out_weight,
        up_weight,
        down_weight,
        first_gain[None],
        first_shift[None],
        out_bias[None],
        second_gain[None],
        second_shift[None],
        down_bias[None],
        up_bias[None],
        qv_bias,
    )
    block_out = from_slots(block, tokens.shape[0], length0, length1)
    input_grad = from_slots(ingrad, tokens.shape[0], length0, length1).astype(F32)
    attn = grads[2].astype(F32)
    return (
        block_out,
        input_grad,
        small[0],
        small[1],
        jnp.transpose(attn[third:].reshape(3, third, width), (2, 0, 1)),
        small[9:11, :third],
        attn[:third],
        small[4],
        small[2],
        small[3],
        grads[1].astype(F32),
        small[8],
        grads[0].astype(F32),
        small[5],
    )


def solution(mesh):
    in_specs = (
        P("dp", None),
        P("dp", None),
        P(),
        P(),
        P(),
        P(),
        P(None, None, "tensor"),
        P(None, "tensor"),
        P("tensor", None),
        P(),
        P(),
        P(),
        P(None, "tensor"),
        P("tensor"),
        P("tensor", None),
        P(),
    )
    out_specs = (
        P("dp", None),
        P("dp", None),
        P(),
        P(),
        P(None, None, "tensor"),
        P(None, "tensor"),
        P("tensor", None),
        P(),
        P(),
        P(),
        P(None, "tensor"),
        P("tensor"),
        P("tensor", None),
        P(),
    )
    return jax.shard_map(
        functools.partial(body, mesh.shape["dp"]), mesh=mesh, in_specs=in_specs, out_specs=out_specs, check_vma=False
    )
```

```python
import functools

import jax
import jax.numpy as jnp
from jax import lax
from jax.experimental import pallas as pl
from jax.experimental.pallas import tpu as pltpu
from jax.sharding import PartitionSpec as P

HD = 64
RES_SMALL = 197
RES_LARGE = 577
SMALL_START = RES_SMALL // 16 * 16
LARGE_START = RES_LARGE // 16 * 16
SLOT = 608
HALF = 304
EPS = 1e-06
MASKED = -1e30
BF = jnp.bfloat16
F32 = jnp.float32
MESH = pl.DeviceIdType.MESH


def dot_nn(a, b):
    return lax.dot_general(a, b, (((1,), (0,)), ((), ())), preferred_element_type=F32)


def dot_nt(a, b):
    return lax.dot_general(a, b, (((1,), (1,)), ((), ())), preferred_element_type=F32)


def dot_tn(a, b):
    return lax.dot_general(a, b, (((0,), (0,)), ((), ())), preferred_element_type=F32)


def normalize(x):
    mean = jnp.mean(x, axis=-1, keepdims=True)
    centered = x - mean
    var = jnp.mean(centered * centered, axis=-1, keepdims=True)
    scale = lax.rsqrt(var + EPS)
    return centered * scale, scale


def norm_back(u, xn, scale):
    return scale * (
        u
        - jnp.mean(u, axis=-1, keepdims=True)
        - xn * jnp.mean(u * xn, axis=-1, keepdims=True)
    )


def fold8(x):
    return jnp.sum(x.reshape(x.shape[0] // 8, 8, x.shape[1]), axis=0)


def flip(index, stride):
    return index + stride - 2 * stride * ((index // stride) % 2)


def row_loop(count, size, unroll, step, init):
    block = size * unroll

    def several(i, carry):
        for j in range(unroll):
            carry = step(pl.multiple_of(i * block + j * size, 16), carry)
        return carry

    carry = lax.fori_loop(0, count // block, several, init)
    for off in range(count // block * block, count, size):
        carry = step(off, carry)
    return carry


def layer_kernel(
    n_dp,
    group,
    lengths,
    tok_h,
    cot_h,
    wqkv_h,
    wout_h,
    wup_h,
    wdown_h,
    g1,
    b1,
    ob,
    g2,
    b2,
    db,
    ub,
    qvb,
    block_h,
    ingrad_h,
    grads_h,
    small_o,
    tok,
    cot,
    wqkv,
    wout,
    wup,
    wdown,
    vec,
    normed,
    qkv,
    att,
    attc,
    attf,
    probs,
    hidden,
    pregrad,
    middle,
    midgrad,
    mg,
    agrad,
    dqkv,
    dacc,
    tmp_a,
    tmp_b,
    acc,
    accv,
    csend,
    crecv,
    ysend,
    yrecv,
    gbuf,
    obuf,
    rx,
    block,
    ingrad,
    smc,
    smr,
    l_sem,
    w_send,
    w_recv,
    a_send,
    a_recv,
    c_send,
    c_recv,
    y_send,
    y_recv,
    g_send,
    g_recv,
    d_send,
    d_recv,
    s_send,
    s_recv,
    *more,
):
    rs, normed2 = more[:12], (more[12:14], more[14:16])
    levels = n_dp.bit_length() - 1
    d = lax.axis_index("dp")
    t = lax.axis_index("tensor")
    core = t % 2
    side = t // 2
    core_peer = (d, flip(t, 1))
    y_peer = (d, flip(t, 2))
    rows, width = tok_h.shape
    third = wout_h.shape[0]
    heads = third // HD

    def dp_peer(level):
        return (flip(d, 2**level), t)

    def local(i, src, dst):
        return pltpu.make_async_copy(src, dst, l_sem.at[i])

    my_quarter = pl.ds(pl.multiple_of(t * third, 16), third)
    its_quarter = pl.ds(pl.multiple_of(flip(t, 2) * third, 16), third)
    loads = [
        local(0, tok_h, tok.at[0:rows]),
        local(1, wqkv_h, wqkv),
        local(2, wout_h, wout.at[my_quarter]),
        local(3, cot_h, hidden.at[0:rows]),
        local(4, wup_h, wup),
        local(5, wdown_h, wdown),
    ]
    for copy in loads:
        copy.start()
    bar = pltpu.get_barrier_semaphore()
    peers = [core_peer, y_peer] + [dp_peer(i) for i in range(levels)]
    for peer in peers:
        pl.semaphore_signal(bar, inc=1, device_id=peer, device_id_type=MESH)

    def look(i, found):
        count, first, second = found
        here = group[i] == d
        first = jnp.where(here & (count == 0), lengths[i], first)
        second = jnp.where(here & (count == 1), lengths[i], second)
        return count + here.astype(jnp.int32), first, second

    zero = jnp.int32(0)
    _, first_len, second_len = lax.fori_loop(0, group.shape[0], look, (zero, zero, zero))
    first_small = first_len == RES_SMALL
    second_skip = jnp.where(first_small, RES_SMALL % 16, RES_LARGE % 16)

    def group_rows(ref, s, off, size):
        small = ref[pl.ds(pl.multiple_of(s * SMALL_START + off, 16), size), :].astype(F32)
        large = ref[pl.ds(pl.multiple_of(s * LARGE_START + off, 16), size), :].astype(F32)
        return jnp.where(first_small, small, large)

    def inside(s, index):
        low = s * second_skip
        return (index >= low) & (index < low + jnp.where(s == 0, first_len, second_len))

    for i, ref in enumerate((g1, b1, ob, g2, b2, db, ub)):
        vec[i : i + 1, :] = ref[...][None, :]
    gain1, shift1, bias_out, gain2, shift2, bias_down, bias_up = (vec.at[i : i + 1] for i in range(7))
    acc[...] = jnp.zeros_like(acc)
    accv[...] = jnp.zeros_like(accv)
    tok[rows:, :] = jnp.zeros((tok.shape[0] - rows, width), BF)

    own, other = 0, HALF
    half_start = (core * HALF, (1 - core) * HALF)
    lane_head = lax.broadcasted_iota(jnp.int32, (1, third), 1) // HD
    zero8 = jnp.zeros((8, width), F32)

    def slot_rows(s, off, size):
        return pl.ds(pl.multiple_of(s * SLOT + off, 16), size)

    def remote(src, dst, send, recv, peer):
        return pltpu.make_async_remote_copy(
            src_ref=src, dst_ref=dst, send_sem=send, recv_sem=recv, device_id=peer, device_id_type=MESH
        )

    def c_copy(s, k):
        return remote(csend, crecv.at[s, k], c_send.at[s, k], c_recv.at[s, k], core_peer)

    def y_copy(s, k):
        return remote(ysend.at[s, k], yrecv.at[s, k], y_send.at[s, k], y_recv.at[s, k], y_peer)

    def norm_copy(s):
        return remote(normed2[s][0], normed2[s][1], g_send.at[s, 0], g_recv.at[s, 0], core_peer)

    def half_copy(ref, s, k):
        mine, its = slot_rows(s, own, HALF), slot_rows(s, other, HALF)
        return remote(ref.at[mine], ref.at[its], g_send.at[s, k], g_recv.at[s, k], core_peer)

    def gather_copy(ref, s, k):
        region = slot_rows(s, half_start[0], HALF)
        return remote(ref.at[region], ref.at[region], g_send.at[s, k], g_recv.at[s, k], core_peer)

    def stage(s, k, part):
        csend[...] = part(other).astype(BF)
        copy = c_copy(s, k)
        copy.start()
        tmp_a[...] = part(own)
        copy.wait()

        def add(off, carry):
            r = pl.ds(off, 16)
            ysend[s, k, r, :] = (tmp_a[r, :] + crecv[s, k, r, :].astype(F32)).astype(BF)
            return carry

        row_loop(HALF, 16, 6, add, 0)
        y_copy(s, k).start()

    def total(s, k, r):
        return ysend[s, k, r, :].astype(F32) + yrecv[s, k, r, :].astype(F32)

    units = [
        (0, width, (0, 1, 2)),
        (width, width, (1, 0, 2)),
        (2 * width, 2 * third, (0, 1, 2)),
        (2 * width + 2 * third, 2 * third, (1, 0, 2)),
    ]

    def bit(level):
        return (d // 2**level) % 2

    def base(u, depth):
        row0, size, order = units[u]
        for i in range(depth):
            row0 = row0 + bit(order[i]) * (size >> (i + 1))
        return row0

    def dp_rs(u, i):
        _, size, order = units[u]
        part = size >> (i + 1)
        src = pl.ds(pl.multiple_of(base(u, i) + (1 - bit(order[i])) * part, 16), part)
        return remote(gbuf.at[src], rs[3 * u + i], d_send.at[u, i], d_recv.at[u, i], dp_peer(order[i]))

    def dp_add(u, i):
        _, size, _ = units[u]
        dp_rs(u, i).wait()
        start = base(u, i + 1)
        out = obuf if i == 2 else gbuf

        def add(off, carry):
            r = pl.ds(pl.multiple_of(start + off, 16), 16)
            out[r, :] = (gbuf[r, :].astype(F32) + rs[3 * u + i][pl.ds(off, 16), :].astype(F32)).astype(BF)
            return carry

        row_loop(size >> (i + 1), 16, 3, add, 0)

    def dp_extra(u):
        row0, size, _ = units[u]
        mine = pl.ds(pl.multiple_of(base(u, 3), 16), size >> 3)
        spot = pl.ds(row0 >> 3, size >> 3)
        for e in range(levels - 3):
            copy = remote(obuf.at[mine], rx.at[e, spot], d_send.at[u, 6 + e], d_recv.at[u, 6 + e], dp_peer(3 + e))
            copy.start()
            copy.wait()
            obuf[mine, :] = (obuf[mine, :].astype(F32) + rx[e, spot, :].astype(F32)).astype(BF)

    def dp_ag(u, i):
        _, size, order = units[u]
        region = pl.ds(pl.multiple_of(base(u, i + 1), 16), size >> (i + 1))
        return remote(obuf.at[region], obuf.at[region], d_send.at[u, 3 + i], d_recv.at[u, 3 + i], dp_peer(order[i]))

    def dp_out(u):
        row0, size, _ = units[u]
        return local(6 + u, obuf.at[row0 : row0 + size], grads_h.at[row0 : row0 + size])

    def advance(u, k):
        if k < 2:
            dp_add(u, k)
            dp_rs(u, k + 1).start()
        elif k == 2:
            dp_add(u, 2)
            dp_extra(u)
            dp_ag(u, 2).start()
        else:
            dp_ag(u, 5 - k).wait()
            if k < 5:
                dp_ag(u, 4 - k).start()
            else:
                dp_out(u).start()

    def serve(*steps):
        for u, k in steps:
            advance(u, k)

    def norm_rows(s):
        for half, start in enumerate(half_start):

            def step(off, carry):
                xn, _ = normalize(group_rows(tok, s, start + off, 16))
                normed[slot_rows(s, half * HALF + off, 16), :] = (xn * gain1[...] + shift1[...]).astype(BF)
                return carry

            row_loop(HALF, 16, 6, step, 0)

    def mask_rows(s):
        for half, start in enumerate(half_start):

            def step(off, carry):
                ok = inside(s, lax.broadcasted_iota(jnp.int32, (16, 1), 0) + (start + off))
                value = group_rows(hidden, s, start + off, 16)
                cot[slot_rows(s, half * HALF + off, 16), :] = jnp.where(ok, value, 0.0).astype(BF)
                return carry

            row_loop(HALF, 16, 6, step, 0)

    loads[0].wait()
    norm_rows(0)
    pl.semaphore_wait(bar, len(peers))
    loads[2].wait()
    w_own = [
        remote(wout.at[my_quarter], wout.at[my_quarter], w_send.at[0], w_recv.at[0], core_peer),
        remote(wout.at[my_quarter], wout.at[my_quarter], w_send.at[1], w_recv.at[1], y_peer),
    ]
    w_pass = remote(wout.at[its_quarter], wout.at[its_quarter], w_send.at[2], w_recv.at[2], core_peer)
    for copy in w_own:
        copy.start()
    loads[1].wait()
    norm_rows(1)

    def a_swap(s):
        return remote(att.at[slot_rows(s, other, HALF)], attc.at[s], a_send.at[s, 0], a_recv.at[s, 0], core_peer)

    def a_copy(s):
        return remote(attf.at[s, side], attf.at[s, side], a_send.at[s, 1], a_recv.at[s, 1], y_peer)

    def forward_attention(s, carry):
        def project(i, carry):
            r = slot_rows(s, i * HALF, HALF)
            x = normed[r, :]
            qkv[0, r, :] = (dot_nt(x, wqkv[0]) + qvb[0:1, :]).astype(BF)
            qkv[1, r, :] = dot_nt(x, wqkv[1]).astype(BF)
            qkv[2, r, :] = (dot_nt(x, wqkv[2]) + qvb[1:2, :]).astype(BF)
            return carry

        lax.fori_loop(0, 2, project, 0)
        whole = slot_rows(s, 0, SLOT)
        key = lax.broadcasted_iota(jnp.int32, (1, SLOT), 1)
        key = key + jnp.where(key < HALF, half_start[0], half_start[1] - HALF)
        key_bias = jnp.where(inside(s, key), 0.0, MASKED)

        def attend(i, carry):
            r = slot_rows(s, i * HALF, HALF)
            for h in range(heads):
                q = jnp.where(lane_head == h, qkv[0, r, :] * HD**-0.5, 0.0).astype(BF)
                scores = dot_nt(q, qkv[1, whole, :]) + key_bias
                exps = jnp.exp(scores - jnp.max(scores, axis=-1, keepdims=True))
                weights = (exps * (1.0 / jnp.sum(exps, axis=-1, keepdims=True))).astype(BF)
                probs[s * heads + h, pl.ds(pl.multiple_of(i * HALF, 16), HALF), :] = weights
                part = dot_nn(weights, qkv[2, whole, :])
                result = part if h == 0 else jnp.where(lane_head == h, part, result)
            att[r, :] = result.astype(BF)
            return carry

        lax.fori_loop(0, 2, attend, 0)
        a_swap(s).start()
        a_swap(s).wait()
        mine, its = att[slot_rows(s, own, HALF), :], attc[s]
        left = jnp.where(core == 0, mine, its)
        right = jnp.where(core == 0, its, mine)
        attf[s, side] = jnp.concatenate([left, right], axis=1)
        a_copy(s).start()
        return carry

    lax.fori_loop(0, 2, forward_attention, 0)
    w_own[1].wait()
    w_pass.start()
    loads[3].wait()
    mask_rows(0)
    mask_rows(1)
    w_own[0].wait()
    w_pass.wait()
    loads[4].wait()
    loads[5].wait()

    def second_norm(s):
        a_copy(s).wait()
        tmp_a[...] = dot_nn(jnp.concatenate([attf[s, 0], attf[s, 1]], axis=1), wout[...])

        def step(off, carry):
            r = pl.ds(off, 16)
            m = tmp_a[r, :] + group_rows(tok, s, half_start[0] + off, 16) + bias_out[...]
            middle[s, r, :] = m
            xn, _ = normalize(m)
            normed2[s][0][r, :] = (xn * gain2[...] + shift2[...]).astype(BF)
            return carry

        row_loop(HALF, 16, 6, step, 0)
        norm_copy(s).start()

    def feed_forward(s):
        second_norm(s)

        def half(start):
            r = slot_rows(s, start, HALF)
            tmp_a[...] = dot_nn(normed2[s][start // HALF][...], wup[...])
            tmp_b[...] = dot_nt(cot[r, :], wdown[...])

            def step(off, sums):
                rr = pl.ds(off, 16)
                g = slot_rows(s, start + off, 16)
                x = tmp_a[rr, :] + bias_up[...]
                phi = 0.5 + 0.5 * lax.erf(x * 0.7071067811865476)
                hidden[g, :] = (x * phi).astype(BF)
                slope = phi + x * (jnp.exp(x * x * -0.5) * 0.3989422804014327)
                low = (tmp_b[rr, :] * slope).astype(BF)
                pregrad[g, :] = low
                return sums + fold8(low.astype(F32))

            acc[6] += row_loop(HALF, 16, 1, step, zero8)

        half(own)
        norm_copy(s).wait()
        half(other)
        stage(s, 0, lambda off: dot_nt(pregrad[slot_rows(s, off, HALF), :], wup[...]))

    feed_forward(0)
    feed_forward(1)

    def weight_grad(u, left, right):
        row0, size, order = units[u]
        for mine in (0, 1):
            off = (bit(order[0]) if mine else 1 - bit(order[0])) * (size // 2)

            columns = left(pl.ds(pl.multiple_of(off, 128), size // 2))
            gbuf[pl.ds(pl.multiple_of(row0 + off, 16), size // 2), :] = dot_tn(columns, right[...]).astype(BF)
            if not mine:
                dp_rs(u, 0).start()

    def norm_columns(columns):
        return jnp.concatenate([ref[:, columns] for refs in normed2 for ref in refs], axis=0)

    weight_grad(0, lambda columns: hidden[:, columns], cot)
    weight_grad(1, norm_columns, pregrad)

    def feed_forward_out(s, carry):
        stage(s, 1, lambda off: dot_nn(hidden[slot_rows(s, off, HALF), :], wdown[...]))
        return carry

    lax.fori_loop(0, 2, feed_forward_out, 0)

    def second_back(s):
        y_copy(s, 0).wait()

        def step(off, sums):
            r = pl.ds(off, 16)
            g = slot_rows(s, own + off, 16)
            n = total(s, 0, r)
            xn, scale = normalize(middle[s, r, :])
            og = cot[g, :].astype(F32)
            m = og + norm_back(n * gain2[...], xn, scale)
            midgrad[s, r, :] = m
            mg[g, :] = m.astype(BF)
            return tuple(a + fold8(b) for a, b in zip(sums, (n * xn, n, m, og), strict=True))

        sums = row_loop(HALF, 16, 3, step, (zero8,) * 4)
        for i in range(4):
            acc[2 + i] += sums[i]
        half_copy(mg, s, 1).start()

    def attention_back(s, services):
        second_back(s)
        half_copy(mg, s, 1).wait()
        whole = slot_rows(s, 0, SLOT)
        agrad[whole, :] = dot_nt(mg[whole, :], wout[my_quarter, :]).astype(BF)
        dacc[...] = jnp.zeros_like(dacc)

        def chunk(i):
            r = slot_rows(s, i * HALF, HALF)
            for h in range(heads):
                mask = lane_head == h
                do = agrad[r, :]
                w = probs[s * heads + h, pl.ds(pl.multiple_of(i * HALF, 16), HALF), :]
                prob_grad = dot_nt(jnp.where(mask, do, 0.0).astype(BF), qkv[2, whole, :])
                p = w.astype(F32)
                inner = jnp.sum(p * prob_grad, axis=-1, keepdims=True)
                score_grad = (p * (prob_grad - inner)).astype(BF)
                part = dot_nn(score_grad, qkv[1, whole, :])
                dq = part if h == 0 else jnp.where(mask, part, dq)
                dacc[0] += jnp.where(mask, dot_tn(score_grad, qkv[0, r, :]), 0.0)
                dacc[1] += jnp.where(mask, dot_tn(w, do), 0.0)
            low = (dq * HD**-0.5).astype(BF)
            dqkv[0, r, :] = low
            accv[0] += fold8(low.astype(F32))

            serve(*services[i])

        chunk(0)
        chunk(1)
        dqkv[1, whole, :] = (dacc[0] * HD**-0.5).astype(BF)
        low = dacc[1].astype(BF)
        dqkv[2, whole, :] = low
        accv[1] += fold8(low.astype(F32))

        def part(off):
            r = slot_rows(s, off, HALF)
            return dot_nn(dqkv[0, r, :], wqkv[0]) + dot_nn(dqkv[1, r, :], wqkv[1]) + dot_nn(dqkv[2, r, :], wqkv[2])

        stage(s, 2, part)

    attention_back(0, (((0, 0),), ((1, 0),)))
    attention_back(1, (((0, 1), (1, 1)), ((0, 2), (1, 2))))

    low0 = 2 * width
    gbuf[low0 : low0 + third, :] = dot_tn(att[...], mg[...]).astype(BF)
    gbuf[low0 + third : low0 + 2 * third, :] = dot_tn(dqkv[0], normed[...]).astype(BF)
    dp_rs(2, 0).start()
    gbuf[low0 + 2 * third : low0 + 3 * third, :] = dot_tn(dqkv[1], normed[...]).astype(BF)
    gbuf[low0 + 3 * third : low0 + 4 * third, :] = dot_tn(dqkv[2], normed[...]).astype(BF)
    dp_rs(3, 0).start()
    serve((0, 3), (1, 3))

    def finish_block(s):
        y_copy(s, 1).wait()

        def step(off, carry):
            r = pl.ds(off, 16)
            block[slot_rows(s, half_start[0] + off, 16), :] = (middle[s, r, :] + total(s, 1, r) + bias_down[...]).astype(BF)
            return carry

        row_loop(HALF, 16, 6, step, 0)
        gather_copy(block, s, 2).start()

    def finish_grad(s):
        y_copy(s, 2).wait()

        def step(off, sums):
            r = pl.ds(off, 16)
            n = total(s, 2, r)
            xn, scale = normalize(group_rows(tok, s, half_start[0] + off, 16))
            ingrad[slot_rows(s, half_start[0] + off, 16), :] = (midgrad[s, r, :] + norm_back(n * gain1[...], xn, scale)).astype(BF)
            return tuple(a + fold8(b) for a, b in zip(sums, (n * xn, n), strict=True))

        sums = row_loop(HALF, 16, 4, step, (zero8,) * 2)
        for i in range(2):
            acc[i] += sums[i]
        gather_copy(ingrad, s, 3).start()

    def assemble(ref):
        def step(off, carry):
            index = lax.broadcasted_iota(jnp.int32, (16, 1), 0) + off

            def two_from(start):
                source = jnp.clip(off - start, 0, SLOT - 16) + SLOT
                return ref[pl.ds(pl.multiple_of(source, 16), 16), :].astype(F32)

            two = jnp.where(first_small, two_from(SMALL_START), two_from(LARGE_START))
            low = jnp.minimum(off, SLOT - 16)
            one = ref[pl.ds(pl.multiple_of(low, 16), 16), :].astype(F32)
            both = jnp.where(index < first_len, one, two)
            ref[pl.ds(off, 16), :] = jnp.where(index < first_len + second_len, both, 0.0).astype(BF)
            return carry

        row_loop(rows, 16, 1, step, 0)

    serve((2, 0), (3, 0))
    finish_block(0)
    serve((0, 4), (1, 4), (2, 1), (3, 1))
    finish_block(1)
    serve((0, 5), (1, 5), (2, 2), (3, 2))
    for s in (0, 1):
        gather_copy(block, s, 2).wait()
    assemble(block)
    out_block = local(10, block.at[0:rows], block_h)
    out_block.start()
    serve((2, 3), (3, 3))
    finish_grad(0)
    serve((2, 4), (3, 4))
    finish_grad(1)

    for i in range(7):
        row = i if i < 6 else 8
        small_o[row : row + 1, :] = jnp.sum(acc[i], axis=0, keepdims=True)
    small_o[6:8, :] = jnp.zeros((2, width), F32)
    small_o[9:16, :] = jnp.zeros((7, width), F32)
    for i in range(2):
        small_o[9 + i : 10 + i, 0:third] = jnp.sum(accv[i], axis=0, keepdims=True)
    copy = remote(small_o.at[0:8], smc, s_send.at[0], s_recv.at[0], core_peer)
    copy.start()
    copy.wait()
    small_o[0:8, :] = small_o[0:8, :] + smc[...]
    copy = remote(small_o, smr.at[0], s_send.at[1], s_recv.at[1], dp_peer(0))
    copy.start()
    for s in (0, 1):
        gather_copy(ingrad, s, 3).wait()
    assemble(ingrad)
    out_grad = local(11, ingrad.at[0:rows], ingrad_h)
    out_grad.start()
    for i in range(levels):
        if i:
            copy = remote(small_o, smr.at[i], s_send.at[1 + i], s_recv.at[1 + i], dp_peer(i))
            copy.start()
        copy.wait()
        small_o[...] = small_o[...] + smr[i]
    serve((2, 5), (3, 5))
    out_block.wait()
    out_grad.wait()
    for u in range(4):
        dp_out(u).wait()


def unpack_kernel(block, ingrad, down, up, out, qkv, small, *outs):
    outs[0][...] = block[...]
    outs[1][...] = ingrad[...].astype(F32)
    outs[2][...] = down[...].astype(F32)
    outs[3][...] = up[...].astype(F32)
    outs[4][...] = out[...].astype(F32)
    outs[5][...] = qkv[...].astype(F32)

    @pl.when(pl.program_id(0) == 0)
    def _():
        for i, row in enumerate((0, 1, 2, 3, 4, 5, 8)):
            outs[6 + i][...] = small[row]
        outs[13][...] = small[9:11, 0 : outs[13].shape[1]]


def call_unpack(block, ingrad, grads, small, third):
    rows, width = block.shape
    steps = 6
    row_block = -(-rows // (16 * steps)) * 16

    def part(size, start):
        return pl.BlockSpec((size, width), lambda i: (start // size + i, 0))

    def whole(shape):
        return pl.BlockSpec(shape, lambda i: (0,) * len(shape))

    big, mid, low = width // steps, 3 * third // steps, third // steps
    shapes = [
        ((rows, width), BF, part(row_block, 0)),
        ((rows, width), F32, part(row_block, 0)),
        ((width, width), F32, part(big, 0)),
        ((width, width), F32, part(big, 0)),
        ((third, width), F32, part(low, 0)),
        ((3 * third, width), F32, part(mid, 0)),
    ]
    shapes += [((width,), F32, whole((width,)))] * 7 + [((2, third), F32, whole((2, third)))]
    return pl.pallas_call(
        unpack_kernel,
        grid=(steps,),
        out_shape=[jax.ShapeDtypeStruct(shape, kind) for shape, kind, _ in shapes],
        in_specs=[
            part(row_block, 0),
            part(row_block, 0),
            part(big, 0),
            part(big, width),
            part(low, 2 * width),
            part(mid, 2 * width + third),
            whole(small.shape),
        ],
        out_specs=[spec for _, _, spec in shapes],
    )(block, ingrad, grads, grads, grads, grads, small)


def call_layer(n_dp, *operands):
    rows, width = operands[2].shape
    third = operands[5].shape[0]
    heads = third // HD
    levels = n_dp.bit_length() - 1
    extra = max(levels - 3, 1)
    slots = 2 * SLOT
    grad_rows = 2 * width + 4 * third
    vmem = pl.BlockSpec(memory_space=pltpu.VMEM)
    smem = pl.BlockSpec(memory_space=pltpu.SMEM)
    hbm = pl.BlockSpec(memory_space=pl.ANY)
    dma = pltpu.SemaphoreType.DMA
    return pl.pallas_call(
        functools.partial(layer_kernel, n_dp),
        out_shape=(
            jax.ShapeDtypeStruct((rows, width), BF),
            jax.ShapeDtypeStruct((rows, width), BF),
            jax.ShapeDtypeStruct((grad_rows, width), BF),
            jax.ShapeDtypeStruct((16, width), F32),
        ),
        in_specs=[smem] * 2 + [hbm] * 6 + [vmem] * 8,
        out_specs=(hbm, hbm, hbm, vmem),
        scratch_shapes=[
            pltpu.VMEM((rows + 16, width), BF),
            pltpu.VMEM((slots, width), BF),
            pltpu.VMEM((3, third, width), BF),
            pltpu.VMEM((4 * third, width), BF),
            pltpu.VMEM((width, width), BF),
            pltpu.VMEM((width, width), BF),
            pltpu.VMEM((8, width), F32),
            pltpu.VMEM((slots, width), BF),
            pltpu.VMEM((3, slots, third), BF),
            pltpu.VMEM((slots, third), BF),
            pltpu.VMEM((2, HALF, third), BF),
            pltpu.VMEM((2, 2, HALF, 2 * third), BF),
            pltpu.VMEM((2 * heads, SLOT, SLOT), BF),
            pltpu.VMEM((slots, width), BF),
            pltpu.VMEM((slots, width), BF),
            pltpu.VMEM((2, HALF, width), F32),
            pltpu.VMEM((2, HALF, width), F32),
            pltpu.VMEM((slots, width), BF),
            pltpu.VMEM((slots, third), BF),
            pltpu.VMEM((3, slots, third), BF),
            pltpu.VMEM((2, SLOT, third), F32),
            pltpu.VMEM((HALF, width), F32),
            pltpu.VMEM((HALF, width), F32),
            pltpu.VMEM((7, 8, width), F32),
            pltpu.VMEM((2, 8, third), F32),
            pltpu.VMEM((HALF, width), BF),
            pltpu.VMEM((2, 3, HALF, width), BF),
            pltpu.VMEM((2, 3, HALF, width), BF),
            pltpu.VMEM((2, 3, HALF, width), BF),
            pltpu.VMEM((grad_rows, width), BF),
            pltpu.VMEM((grad_rows, width), BF),
            pltpu.VMEM((extra, grad_rows // 8, width), BF),
            pltpu.VMEM((slots, width), BF),
            pltpu.VMEM((slots, width), BF),
            pltpu.VMEM((8, width), F32),
            pltpu.VMEM((levels, 16, width), F32),
            dma((12,)),
            dma((3,)),
            dma((3,)),
            dma((2, 2)),
            dma((2, 2)),
            dma((2, 3)),
            dma((2, 3)),
            dma((2, 3)),
            dma((2, 3)),
            dma((2, 4)),
            dma((2, 4)),
            dma((4, 6 + extra)),
            dma((4, 6 + extra)),
            dma((1 + levels,)),
            dma((1 + levels,)),
        ]
        + [pltpu.VMEM((size >> (i + 1), width), BF) for size in (width, width, 2 * third, 2 * third) for i in range(3)]
        + [pltpu.VMEM((HALF, width), BF)] * 4,
        compiler_params=pltpu.CompilerParams(
            collective_id=0, has_side_effects=True, vmem_limit_bytes=67043328
        ),
    )(*operands)


def body(
    n_dp,
    tokens,
    cotangent,
    image_group,
    image_length,
    first_gain,
    first_shift,
    qkv_weight,
    qv_bias,
    out_weight,
    out_bias,
    second_gain,
    second_shift,
    up_weight,
    up_bias,
    down_weight,
    down_bias,
):
    third = out_weight.shape[0]
    width = tokens.shape[1]
    block, ingrad, grads, small = call_layer(
        n_dp,
        image_group,
        image_length,
        tokens,
        cotangent,
        jnp.transpose(qkv_weight, (1, 2, 0)),
        out_weight,
        up_weight,
        down_weight,
        first_gain,
        first_shift,
        out_bias,
        second_gain,
        second_shift,
        down_bias,
        up_bias,
        qv_bias,
    )
    outs = call_unpack(block, ingrad, grads, small, third)
    block_out, input_grad, down_grad, up_grad, out_grad, qkv_grad = outs[:6]
    g1, b1, g2, b2, out_bias_grad, down_bias_grad, up_bias_grad, qv_bias_grad = outs[6:]
    return (
        block_out,
        input_grad,
        g1,
        b1,
        jnp.transpose(qkv_grad.reshape(3, third, width), (2, 0, 1)),
        qv_bias_grad,
        out_grad,
        out_bias_grad,
        g2,
        b2,
        up_grad,
        up_bias_grad,
        down_grad,
        down_bias_grad,
    )


def solution(mesh):
    in_specs = (
        P("dp", None),
        P("dp", None),
        P(),
        P(),
        P(),
        P(),
        P(None, None, "tensor"),
        P(None, "tensor"),
        P("tensor", None),
        P(),
        P(),
        P(),
        P(None, "tensor"),
        P("tensor"),
        P("tensor", None),
        P(),
    )
    out_specs = (
        P("dp", None),
        P("dp", None),
        P(),
        P(),
        P(None, None, "tensor"),
        P(None, "tensor"),
        P("tensor", None),
        P(),
        P(),
        P(),
        P(None, "tensor"),
        P("tensor"),
        P("tensor", None),
        P(),
    )
    return jax.shard_map(
        functools.partial(body, mesh.shape["dp"]), mesh=mesh, in_specs=in_specs, out_specs=out_specs, check_vma=False
    )
```

```python
import functools

import jax
import jax.numpy as jnp
from jax import lax
from jax.experimental import pallas as pl
from jax.experimental.pallas import tpu as pltpu
from jax.sharding import PartitionSpec as P

HD = 64
RES_SMALL = 197
RES_LARGE = 577
SMALL_START = RES_SMALL // 16 * 16
LARGE_START = RES_LARGE // 16 * 16
SLOT = 608
HALF = 304
EPS = 1e-06
MASKED = -1e30
BF = jnp.bfloat16
F32 = jnp.float32
MESH = pl.DeviceIdType.MESH


def dot_nn(a, b):
    return lax.dot_general(a, b, (((1,), (0,)), ((), ())), preferred_element_type=F32)


def dot_nt(a, b):
    return lax.dot_general(a, b, (((1,), (1,)), ((), ())), preferred_element_type=F32)


def dot_tn(a, b):
    return lax.dot_general(a, b, (((0,), (0,)), ((), ())), preferred_element_type=F32)


def normalize(x):
    mean = jnp.mean(x, axis=-1, keepdims=True)
    centered = x - mean
    var = jnp.mean(centered * centered, axis=-1, keepdims=True)
    scale = lax.rsqrt(var + EPS)
    return centered * scale, scale


def norm_back(u, xn, scale):
    return scale * (
        u
        - jnp.mean(u, axis=-1, keepdims=True)
        - xn * jnp.mean(u * xn, axis=-1, keepdims=True)
    )


def fold8(x):
    return jnp.sum(x.reshape(x.shape[0] // 8, 8, x.shape[1]), axis=0)


def flip(index, stride):
    return index + stride - 2 * stride * ((index // stride) % 2)


def row_loop(count, size, unroll, step, init):
    block = size * unroll

    def several(i, carry):
        for j in range(unroll):
            carry = step(pl.multiple_of(i * block + j * size, 16), carry)
        return carry

    carry = lax.fori_loop(0, count // block, several, init)
    for off in range(count // block * block, count, size):
        carry = step(off, carry)
    return carry


FIRST, SECOND = (0, 1, 2), (1, 0, 2)
ORDERS = (FIRST, SECOND, FIRST, FIRST, FIRST, FIRST, FIRST, SECOND)
PLAN = {
    "back0": ((0, 0), (1, 0)),
    "head010": ((2, 0), (0, 1)),
    "back1": (("early", 0),),
    "head021": ((2, 1), (3, 0)),
    "out": (("early", 1), (1, 1), (0, 2)),
    "head101": (("early", 2),),
    "head110": ((4, 0), (3, 1), (2, 2)),
    "head111": (("early", 3),),
    "head120": ((5, 0),),
    "head121": ((0, 3), ("early", 4)),
    "heads": ((1, 2), (4, 1), (6, 0)),
    "block": ((3, 2), (2, 3), (0, 4), (5, 1), (4, 2)),
    "grad0": ((1, 3), (7, 0), (5, 2), (6, 1), (2, 4), (3, 3), (7, 1)),
    "grad1": (
        (6, 2),
        (4, 3),
        ("late", 1),
        (7, 2),
        (3, 4),
        (1, 4),
        (5, 3),
        (4, 4),
        ("late", 2),
        (7, 3),
        (6, 3),
        ("late", 3),
        (5, 4),
        ("late", 4),
        (7, 4),
        (6, 4),
    ),
}


def dp_units(width, third):
    units, start = [], 0
    for size, order in zip((width // 2,) * 4 + (third,) * 4, ORDERS, strict=True):
        units.append((start, size, order))
        start += size
    return units


def layer_kernel(
    n_dp,
    group,
    lengths,
    tok_h,
    cot_h,
    wqkv_h,
    wout_h,
    wup_h,
    wdown_h,
    g1,
    b1,
    ob,
    g2,
    b2,
    db,
    ub,
    qvb,
    block_h,
    ingrad_h,
    grads_h,
    small_o,
    tok,
    cot,
    wqkv,
    wout,
    wup,
    wdown,
    vec,
    normed,
    qkv,
    att,
    attc,
    attf,
    probs,
    hidden,
    pregrad,
    middle,
    midgrad,
    keep,
    agrad,
    dhead,
    wstack,
    sgrad,
    slope,
    tmp_a,
    acc,
    acch,
    csend,
    crecv,
    ysend,
    yrecv,
    gbuf,
    obuf,
    rx,
    early,
    late,
    block,
    ingrad,
    early_c,
    early_r,
    late_c,
    late_r,
    l_sem,
    w_send,
    w_recv,
    a_send,
    a_recv,
    c_send,
    c_recv,
    y_send,
    y_recv,
    g_send,
    g_recv,
    d_send,
    d_recv,
    s_send,
    s_recv,
    *more,
):
    rs, normed2, mg = more[:24], (more[24:26], more[26:28]), (more[28:30], more[30:32])
    levels = n_dp.bit_length() - 1
    d = lax.axis_index("dp")
    t = lax.axis_index("tensor")
    core = t % 2
    side = t // 2
    core_peer = (d, flip(t, 1))
    y_peer = (d, flip(t, 2))
    rows, width = tok_h.shape
    third = wout_h.shape[0]
    heads = third // HD

    def dp_peer(level):
        return (flip(d, 2**level), t)

    def local(i, src, dst):
        return pltpu.make_async_copy(src, dst, l_sem.at[i])

    my_quarter = pl.ds(pl.multiple_of(t * third, 16), third)
    its_quarter = pl.ds(pl.multiple_of(flip(t, 2) * third, 16), third)
    loads = [
        local(0, tok_h, tok.at[0:rows]),
        local(1, wqkv_h, wqkv),
        local(2, wout_h, wout.at[my_quarter]),
        local(3, cot_h, hidden.at[0:rows]),
        local(4, wup_h, wup),
        local(5, wdown_h, wdown),
    ]
    for copy in loads:
        copy.start()
    bar = pltpu.get_barrier_semaphore()
    peers = [core_peer, y_peer] + [dp_peer(i) for i in range(levels)]
    for peer in peers:
        pl.semaphore_signal(bar, inc=1, device_id=peer, device_id_type=MESH)

    def look(i, found):
        count, first, second = found
        here = group[i] == d
        first = jnp.where(here & (count == 0), lengths[i], first)
        second = jnp.where(here & (count == 1), lengths[i], second)
        return count + here.astype(jnp.int32), first, second

    zero = jnp.int32(0)
    _, first_len, second_len = lax.fori_loop(0, group.shape[0], look, (zero, zero, zero))
    first_small = first_len == RES_SMALL
    second_skip = jnp.where(first_small, RES_SMALL % 16, RES_LARGE % 16)

    def group_rows(ref, s, off, size):
        small = ref[pl.ds(pl.multiple_of(s * SMALL_START + off, 16), size), :].astype(F32)
        large = ref[pl.ds(pl.multiple_of(s * LARGE_START + off, 16), size), :].astype(F32)
        return jnp.where(first_small, small, large)

    def inside(s, index):
        low = s * second_skip
        return (index >= low) & (index < low + jnp.where(s == 0, first_len, second_len))

    for i, ref in enumerate((g1, b1, ob, g2, b2, db, ub)):
        vec[i : i + 1, :] = ref[...][None, :]
    gain1, shift1, bias_out, gain2, shift2, bias_down, bias_up = (vec.at[i : i + 1] for i in range(7))
    acc[...] = jnp.zeros_like(acc)
    acch[...] = jnp.zeros_like(acch)
    tok[rows:, :] = jnp.zeros((tok.shape[0] - rows, width), BF)

    own, other = 0, HALF
    half_start = (core * HALF, (1 - core) * HALF)
    zero8 = jnp.zeros((8, width), F32)

    def slot_rows(s, off, size):
        return pl.ds(pl.multiple_of(s * SLOT + off, 16), size)

    def remote(src, dst, send, recv, peer):
        return pltpu.make_async_remote_copy(
            src_ref=src, dst_ref=dst, send_sem=send, recv_sem=recv, device_id=peer, device_id_type=MESH
        )

    def c_copy(s, k):
        return remote(csend, crecv.at[s, k], c_send.at[s, k], c_recv.at[s, k], core_peer)

    def y_copy(s, k):
        return remote(ysend.at[s, k], yrecv.at[s, k], y_send.at[s, k], y_recv.at[s, k], y_peer)

    def half_copy(refs, s, k):
        return remote(refs[s][0], refs[s][1], g_send.at[s, k], g_recv.at[s, k], core_peer)

    def gather_copy(ref, s, k):
        region = slot_rows(s, half_start[0], HALF)
        return remote(ref.at[region], ref.at[region], g_send.at[s, k], g_recv.at[s, k], core_peer)

    def begin(s, k, part):
        csend[...] = part(other).astype(BF)
        c_copy(s, k).start()
        keep[...] = part(own)

    def end(s, k):
        c_copy(s, k).wait()

        def add(off, carry):
            r = pl.ds(off, 16)
            ysend[s, k, r, :] = (keep[r, :] + crecv[s, k, r, :].astype(F32)).astype(BF)
            return carry

        row_loop(HALF, 16, 6, add, 0)
        y_copy(s, k).start()

    def total(s, k, r):
        return ysend[s, k, r, :].astype(F32) + yrecv[s, k, r, :].astype(F32)

    units = dp_units(width, third)

    def bit(level):
        return (d // 2**level) % 2

    def base(u, depth):
        row0, size, order = units[u]
        for i in range(depth):
            row0 = row0 + bit(order[i]) * (size >> (i + 1))
        return row0

    def region(u, depth):
        return pl.ds(pl.multiple_of(base(u, depth), 16), units[u][1] >> depth)

    def dp_rs(u, i):
        _, size, order = units[u]
        part = size >> (i + 1)
        src = pl.ds(pl.multiple_of(base(u, i) + (1 - bit(order[i])) * part, 16), part)
        return remote(gbuf.at[src], rs[3 * u + i], d_send.at[u, i], d_recv.at[u, i], dp_peer(order[i]))

    def dp_swap(u):
        return remote(gbuf.at[region(u, 2)], rs[3 * u + 2], d_send.at[u, 2], d_recv.at[u, 2], dp_peer(units[u][2][2]))

    def dp_ag(u, i):
        mine = obuf.at[region(u, i + 1)]
        return remote(mine, mine, d_send.at[u, 3 + i], d_recv.at[u, 3 + i], dp_peer(units[u][2][i]))

    def dp_add(u, i, out):
        start = base(u, min(i + 1, 2))

        def add(off, carry):
            r = pl.ds(pl.multiple_of(start + off, 16), 16)
            out[r, :] = (gbuf[r, :].astype(F32) + rs[3 * u + i][pl.ds(off, 16), :].astype(F32)).astype(BF)
            return carry

        row_loop(units[u][1] >> min(i + 1, 2), 16, 3, add, 0)

    def dp_further(u):
        spot = pl.ds(units[u][0] >> 2, units[u][1] >> 2)
        for e in range(levels - 3):
            mine = region(u, 2)
            copy = remote(obuf.at[mine], rx.at[e, spot], d_send.at[u, 5 + e], d_recv.at[u, 5 + e], dp_peer(3 + e))
            copy.start()
            copy.wait()
            obuf[mine, :] = (obuf[mine, :].astype(F32) + rx[e, spot, :].astype(F32)).astype(BF)

    def dp_out(u):
        row0, size, _ = units[u]
        return local(6 + u, obuf.at[row0 : row0 + size], grads_h.at[row0 : row0 + size])

    def advance(u, k):
        if k == 0:
            dp_rs(u, 0).wait()
            dp_add(u, 0, gbuf)
            dp_rs(u, 1).start()
        elif k == 1:
            dp_rs(u, 1).wait()
            dp_add(u, 1, gbuf)
            dp_swap(u).start()
        elif k == 2:
            dp_swap(u).wait()
            dp_add(u, 2, obuf)
            dp_further(u)
            dp_ag(u, 1).start()
        elif k == 3:
            dp_ag(u, 1).wait()
            dp_ag(u, 0).start()
        else:
            dp_ag(u, 0).wait()
            dp_out(u).start()

    def serve(place):
        for u, k in PLAN.get(place, ()):
            if u == "early":
                early_step(k)
            elif u == "late":
                late_step(k)
            else:
                advance(u, k)

    def exchange(buf, landing, sem, peer):
        return remote(buf, landing, s_send.at[sem], s_recv.at[sem], peer)

    def early_step(k):
        if k == 0:
            early[...] = jnp.zeros_like(early)
            for i in range(4):
                early[i : i + 1, :] = jnp.sum(acc[2 + i], axis=0, keepdims=True)
            exchange(early, early_c, 0, core_peer).start()
            return
        landing = early_c if k == 1 else early_r.at[k - 2]
        exchange(early, landing, k - 1, core_peer if k == 1 else dp_peer(k - 2)).wait()
        early[...] = early[...] + landing[...]
        if k == 1:
            early[4:5, :] = jnp.sum(acc[6], axis=0, keepdims=True)
        if k <= levels:
            exchange(early, early_r.at[k - 1], k, dp_peer(k - 1)).start()

    tiles = width // 128

    def late_step(k):
        first = 1 + levels
        if k == 0:
            late[...] = jnp.zeros_like(late)
            for i in range(2):
                row = jnp.sum(acc[i], axis=0, keepdims=True)
                for j in range(tiles):
                    late[i * tiles + j : i * tiles + j + 1, :] = row[:, j * 128 : (j + 1) * 128]
            exchange(late, late_c, first, core_peer).start()
            return
        landing = late_c if k == 1 else late_r.at[k - 2]
        exchange(late, landing, first + k - 1, core_peer if k == 1 else dp_peer(k - 2)).wait()
        late[...] = late[...] + landing[...]
        if k == 1:
            for h in range(heads):
                row = jnp.sum(acch[h], axis=0, keepdims=True)
                late[2 * tiles + h : 2 * tiles + h + 1, 0:HD] = row[:, 0:HD]
                late[2 * tiles + h : 2 * tiles + h + 1, HD : 2 * HD] = row[:, 2 * HD : 3 * HD]
        if k <= levels:
            exchange(late, late_r.at[k - 1], first + k, dp_peer(k - 1)).start()

    def norm_rows(s):
        for half, start in enumerate(half_start):

            def step(off, carry):
                xn, _ = normalize(group_rows(tok, s, start + off, 16))
                normed[slot_rows(s, half * HALF + off, 16), :] = (xn * gain1[...] + shift1[...]).astype(BF)
                return carry

            row_loop(HALF, 16, 6, step, 0)

    def mask_rows(s):
        for half, start in enumerate(half_start):

            def step(off, carry):
                ok = inside(s, lax.broadcasted_iota(jnp.int32, (16, 1), 0) + (start + off))
                value = group_rows(hidden, s, start + off, 16)
                cot[slot_rows(s, half * HALF + off, 16), :] = jnp.where(ok, value, 0.0).astype(BF)
                return carry

            row_loop(HALF, 16, 6, step, 0)

    loads[0].wait()
    norm_rows(0)
    pl.semaphore_wait(bar, len(peers))
    loads[2].wait()
    w_own = [
        remote(wout.at[my_quarter], wout.at[my_quarter], w_send.at[0], w_recv.at[0], core_peer),
        remote(wout.at[my_quarter], wout.at[my_quarter], w_send.at[1], w_recv.at[1], y_peer),
    ]
    w_pass = remote(wout.at[its_quarter], wout.at[its_quarter], w_send.at[2], w_recv.at[2], core_peer)
    for copy in w_own:
        copy.start()
    loads[1].wait()
    norm_rows(1)
    for h in range(heads):
        for j in range(3):
            wstack[h, j * HD : (j + 1) * HD, :] = wqkv[j, h * HD : (h + 1) * HD, :]

    def a_swap(s):
        return remote(att.at[slot_rows(s, other, HALF)], attc.at[s], a_send.at[s, 0], a_recv.at[s, 0], core_peer)

    def a_copy(s):
        return remote(attf.at[s, side], attf.at[s, side], a_send.at[s, 1], a_recv.at[s, 1], y_peer)

    def project(s):
        def half(i, carry):
            r = slot_rows(s, i * HALF, HALF)
            x = normed[r, :]
            qkv[0, r, :] = (dot_nt(x, wqkv[0]) + qvb[0:1, :]).astype(BF)
            qkv[1, r, :] = dot_nt(x, wqkv[1]).astype(BF)
            qkv[2, r, :] = (dot_nt(x, wqkv[2]) + qvb[1:2, :]).astype(BF)
            return carry

        lax.fori_loop(0, 2, half, 0)

    def attend(s):
        whole = slot_rows(s, 0, SLOT)
        key = lax.broadcasted_iota(jnp.int32, (1, SLOT), 1)
        key = key + jnp.where(key < HALF, half_start[0], half_start[1] - HALF)
        key_bias = jnp.where(inside(s, key), 0.0, MASKED)

        def half(i, carry):
            r = slot_rows(s, i * HALF, HALF)
            for h in range(heads):
                lanes = slice(h * HD, (h + 1) * HD)
                q = (qkv[0, r, lanes] * HD**-0.5).astype(BF)
                scores = dot_nt(q, qkv[1, whole, lanes]) + key_bias
                exps = jnp.exp(scores - jnp.max(scores, axis=-1, keepdims=True))
                weights = (exps * (1.0 / jnp.sum(exps, axis=-1, keepdims=True))).astype(BF)
                probs[s * heads + h, pl.ds(pl.multiple_of(i * HALF, 16), HALF), :] = weights
                att[r, lanes] = dot_nn(weights, qkv[2, whole, lanes]).astype(BF)
            return carry

        lax.fori_loop(0, 2, half, 0)
        a_swap(s).start()

    def join(s):
        a_swap(s).wait()
        mine, its = att[slot_rows(s, own, HALF), :], attc[s]
        left = jnp.where(core == 0, mine, its)
        right = jnp.where(core == 0, its, mine)
        attf[s, side] = jnp.concatenate([left, right], axis=1)
        a_copy(s).start()

    project(0)
    attend(0)
    project(1)
    join(0)
    attend(1)
    w_own[1].wait()
    w_pass.start()
    loads[3].wait()
    mask_rows(0)
    join(1)
    mask_rows(1)
    w_own[0].wait()
    w_pass.wait()
    loads[4].wait()
    loads[5].wait()

    def second_norm(s):
        a_copy(s).wait()
        tmp_a[...] = dot_nn(jnp.concatenate([attf[s, 0], attf[s, 1]], axis=1), wout[...])

        def step(off, carry):
            r = pl.ds(off, 16)
            m = tmp_a[r, :] + group_rows(tok, s, half_start[0] + off, 16) + bias_out[...]
            middle[s, r, :] = m
            xn, _ = normalize(m)
            normed2[s][0][r, :] = (xn * gain2[...] + shift2[...]).astype(BF)
            return carry

        row_loop(HALF, 16, 6, step, 0)
        half_copy(normed2, s, 0).start()

    def up_half(s, half):
        tmp_a[...] = dot_nn(normed2[s][half][...], wup[...])

        def step(off, carry):
            g = slot_rows(s, half * HALF + off, 16)
            x = tmp_a[pl.ds(off, 16), :] + bias_up[...]
            phi = 0.5 + 0.5 * lax.erf(x * 0.7071067811865476)
            hidden[g, :] = (x * phi).astype(BF)
            slope[g, :] = phi + x * (jnp.exp(x * x * -0.5) * 0.3989422804014327)
            return carry

        row_loop(HALF, 16, 2, step, 0)

    def back_half(s, half):
        tmp_a[...] = dot_nt(cot[slot_rows(s, half * HALF, HALF), :], wdown[...])

        def step(off, sums):
            g = slot_rows(s, half * HALF + off, 16)
            low = (tmp_a[pl.ds(off, 16), :] * slope[g, :]).astype(BF)
            pregrad[g, :] = low
            return sums + fold8(low.astype(F32))

        acc[6] += row_loop(HALF, 16, 6, step, zero8)

    def unit_grad(u, left, right):
        row0, size, _ = units[u]
        gbuf[row0 : row0 + size, :] = dot_tn(left, right[...]).astype(BF)
        dp_rs(u, 0).start()

    def norm_columns(columns):
        return jnp.concatenate([ref[:, columns] for refs in normed2 for ref in refs], axis=0)

    lower, upper = slice(0, width // 2), slice(width // 2, width)
    def norm_part(s):
        begin(s, 0, lambda off: dot_nt(pregrad[slot_rows(s, off, HALF), :], wup[...]))

    def out_part(s):
        begin(s, 1, lambda off: dot_nn(hidden[slot_rows(s, off, HALF), :], wdown[...]))

    second_norm(0)
    up_half(0, 0)
    half_copy(normed2, 0, 0).wait()
    up_half(0, 1)
    back_half(0, 1)
    back_half(0, 0)
    norm_part(0)
    second_norm(1)
    end(0, 0)
    up_half(1, 0)
    half_copy(normed2, 1, 0).wait()
    up_half(1, 1)
    unit_grad(0, hidden[:, lower], cot)
    unit_grad(1, hidden[:, upper], cot)
    back_half(1, 1)
    back_half(1, 0)
    norm_part(1)
    unit_grad(2, norm_columns(lower), pregrad)
    end(1, 0)
    out_part(0)
    unit_grad(3, norm_columns(upper), pregrad)
    end(0, 1)
    out_part(1)

    def second_back(s):
        y_copy(s, 0).wait()

        def step(off, sums):
            r = pl.ds(off, 16)
            g = slot_rows(s, own + off, 16)
            n = total(s, 0, r)
            xn, scale = normalize(middle[s, r, :])
            og = cot[g, :].astype(F32)
            m = og + norm_back(n * gain2[...], xn, scale)
            midgrad[s, r, :] = m
            mg[s][0][r, :] = m.astype(BF)
            return tuple(a + fold8(b) for a, b in zip(sums, (n * xn, n, m, og), strict=True))

        sums = row_loop(HALF, 16, 3, step, (zero8,) * 4)
        for i in range(4):
            acc[2 + i] += sums[i]
        half_copy(mg, s, 1).start()

    def head_back(s, h):
        whole = slot_rows(s, 0, SLOT)
        lanes = slice(h * HD, (h + 1) * HD)
        keys, values = qkv[1, whole, lanes], qkv[2, whole, lanes]
        for c in (0, 1):
            r = slot_rows(s, c * HALF, HALF)
            part = slice(c * HALF, (c + 1) * HALF)
            p = probs[s * heads + h, part, :].astype(F32)
            prob_grad = dot_nt(agrad[r, lanes], values)
            inner = jnp.sum(p * prob_grad, axis=-1, keepdims=True)
            sgrad[part, :] = (p * (prob_grad - inner)).astype(BF)
            dhead[h, r, 0:HD] = (dot_nn(sgrad[part, :], keys) * HD**-0.5).astype(BF)
            serve(f"head{s}{h}{c}")
        dhead[h, whole, HD : 2 * HD] = (dot_tn(sgrad[...], qkv[0, whole, lanes]) * HD**-0.5).astype(BF)
        dhead[h, whole, 2 * HD : 3 * HD] = dot_tn(probs[s * heads + h], agrad[whole, lanes]).astype(BF)
        acch[h] += fold8(dhead[h, whole, :].astype(F32))

    def attended_grad(s):
        half_copy(mg, s, 1).wait()
        agrad[slot_rows(s, 0, SLOT), :] = dot_nt(
            jnp.concatenate([mg[s][0][...], mg[s][1][...]], axis=0), wout[my_quarter, :]
        ).astype(BF)

    def projected(s):
        def part(off):
            r = slot_rows(s, off, HALF)
            return sum(dot_nn(dhead[h, r, :], wstack[h]) for h in range(heads))

        begin(s, 2, part)

    second_back(0)
    end(1, 1)
    serve("back0")
    attended_grad(0)
    for h in range(heads - 1):
        head_back(0, h)
    second_back(1)
    serve("back1")
    head_back(0, heads - 1)
    projected(0)
    attended_grad(1)
    end(0, 2)
    all_mg = jnp.concatenate([ref[...] for refs in mg for ref in refs], axis=0)
    gbuf[2 * width : 2 * width + third, :] = dot_tn(att[...], all_mg).astype(BF)
    dp_rs(4, 0).start()
    serve("out")
    for h in range(heads):
        head_back(1, h)
        if h == heads - 1:
            projected(1)
        unit_grad(5 + h, dhead[h], normed)
    serve("heads")
    end(1, 2)

    def finish_block(s):
        y_copy(s, 1).wait()

        def step(off, carry):
            r = pl.ds(off, 16)
            block[slot_rows(s, half_start[0] + off, 16), :] = (middle[s, r, :] + total(s, 1, r) + bias_down[...]).astype(BF)
            return carry

        row_loop(HALF, 16, 6, step, 0)
        gather_copy(block, s, 2).start()

    def finish_grad(s):
        y_copy(s, 2).wait()

        def step(off, sums):
            r = pl.ds(off, 16)
            n = total(s, 2, r)
            xn, scale = normalize(group_rows(tok, s, half_start[0] + off, 16))
            ingrad[slot_rows(s, half_start[0] + off, 16), :] = (midgrad[s, r, :] + norm_back(n * gain1[...], xn, scale)).astype(BF)
            return tuple(a + fold8(b) for a, b in zip(sums, (n * xn, n), strict=True))

        sums = row_loop(HALF, 16, 4, step, (zero8,) * 2)
        for i in range(2):
            acc[i] += sums[i]
        gather_copy(ingrad, s, 3).start()

    def assemble(ref):
        def step(off, carry):
            index = lax.broadcasted_iota(jnp.int32, (16, 1), 0) + off

            def two_from(start):
                source = jnp.clip(off - start, 0, SLOT - 16) + SLOT
                return ref[pl.ds(pl.multiple_of(source, 16), 16), :].astype(F32)

            two = jnp.where(first_small, two_from(SMALL_START), two_from(LARGE_START))
            low = jnp.minimum(off, SLOT - 16)
            one = ref[pl.ds(pl.multiple_of(low, 16), 16), :].astype(F32)
            both = jnp.where(index < first_len, one, two)
            ref[pl.ds(off, 16), :] = jnp.where(index < first_len + second_len, both, 0.0).astype(BF)
            return carry

        row_loop(rows, 16, 1, step, 0)

    finish_block(0)
    finish_block(1)
    for s in (0, 1):
        gather_copy(block, s, 2).wait()
    assemble(block)
    out_block = local(14, block.at[0:rows], block_h)
    out_block.start()
    serve("block")
    finish_grad(0)
    serve("grad0")
    finish_grad(1)
    late_step(0)
    for s in (0, 1):
        gather_copy(ingrad, s, 3).wait()
    assemble(ingrad)
    out_grad = local(15, ingrad.at[0:rows], ingrad_h)
    out_grad.start()
    serve("grad1")
    for k in range(5, levels + 2):
        early_step(k)
        late_step(k)

    small_o[...] = jnp.zeros_like(small_o)
    for i in range(2):
        for j in range(tiles):
            small_o[i : i + 1, j * 128 : (j + 1) * 128] = late[i * tiles + j : i * tiles + j + 1, :]
    small_o[2:6, :] = early[0:4, :]
    small_o[8:9, :] = early[4:5, :]
    for h in range(heads):
        row = late[2 * tiles + h : 2 * tiles + h + 1, :]
        small_o[9:10, h * HD : (h + 1) * HD] = row[:, 0:HD]
        small_o[10:11, h * HD : (h + 1) * HD] = row[:, HD : 2 * HD]
    out_block.wait()
    out_grad.wait()
    for u in range(len(units)):
        dp_out(u).wait()


def unpack_kernel(block, ingrad, down, up, out, qkv0, qkv1, qkv2, small, *outs):
    outs[0][...] = block[...]
    outs[1][...] = ingrad[...].astype(F32)
    outs[2][...] = down[...].astype(F32)
    outs[3][...] = up[...].astype(F32)
    outs[4][...] = out[...].astype(F32)
    for i, qkv in enumerate((qkv0, qkv1, qkv2)):
        rows = qkv.shape[0]
        outs[5][i * rows : (i + 1) * rows, :] = qkv[...].astype(F32)

    @pl.when(pl.program_id(0) == 0)
    def _():
        for i, row in enumerate((0, 1, 2, 3, 4, 5, 8)):
            outs[6 + i][...] = small[row]
        outs[13][...] = small[9:11, 0 : outs[13].shape[1]]


def call_unpack(block, ingrad, grads, small, third):
    rows, width = block.shape
    steps = 6
    row_block = -(-rows // (16 * steps)) * 16

    def part(size, start):
        return pl.BlockSpec((size, width), lambda i: (start // size + i, 0))

    def whole(shape):
        return pl.BlockSpec(shape, lambda i: (0,) * len(shape))

    big, mid, low = width // steps, 3 * third // steps, third // steps
    piece = mid // 3
    per_head = HD // piece

    def qkv_part(b, i):
        m = 3 * i + b
        kind, rest = m // (third // piece), m % (third // piece)
        head, low_part = rest // per_head, rest % per_head
        return (2 * width + third) // piece + (head * 3 + kind) * per_head + low_part, 0

    shapes = [
        ((rows, width), BF, part(row_block, 0)),
        ((rows, width), F32, part(row_block, 0)),
        ((width, width), F32, part(big, 0)),
        ((width, width), F32, part(big, 0)),
        ((third, width), F32, part(low, 0)),
        ((3 * third, width), F32, part(mid, 0)),
    ]
    shapes += [((width,), F32, whole((width,)))] * 7 + [((2, third), F32, whole((2, third)))]
    return pl.pallas_call(
        unpack_kernel,
        grid=(steps,),
        out_shape=[jax.ShapeDtypeStruct(shape, kind) for shape, kind, _ in shapes],
        in_specs=[
            part(row_block, 0),
            part(row_block, 0),
            part(big, 0),
            part(big, width),
            part(low, 2 * width),
            *(pl.BlockSpec((piece, width), functools.partial(qkv_part, b)) for b in range(3)),
            whole(small.shape),
        ],
        out_specs=[spec for _, _, spec in shapes],
    )(block, ingrad, grads, grads, grads, grads, grads, grads, small)


def call_layer(n_dp, *operands):
    rows, width = operands[2].shape
    third = operands[5].shape[0]
    heads = third // HD
    levels = n_dp.bit_length() - 1
    extra = max(levels - 3, 1)
    slots = 2 * SLOT
    grad_rows = 2 * width + 4 * third
    vmem = pl.BlockSpec(memory_space=pltpu.VMEM)
    smem = pl.BlockSpec(memory_space=pltpu.SMEM)
    hbm = pl.BlockSpec(memory_space=pl.ANY)
    dma = pltpu.SemaphoreType.DMA
    return pl.pallas_call(
        functools.partial(layer_kernel, n_dp),
        out_shape=(
            jax.ShapeDtypeStruct((rows, width), BF),
            jax.ShapeDtypeStruct((rows, width), BF),
            jax.ShapeDtypeStruct((grad_rows, width), BF),
            jax.ShapeDtypeStruct((16, width), F32),
        ),
        in_specs=[smem] * 2 + [hbm] * 6 + [vmem] * 8,
        out_specs=(hbm, hbm, hbm, vmem),
        scratch_shapes=[
            pltpu.VMEM((rows + 16, width), BF),
            pltpu.VMEM((slots, width), BF),
            pltpu.VMEM((3, third, width), BF),
            pltpu.VMEM((4 * third, width), BF),
            pltpu.VMEM((width, width), BF),
            pltpu.VMEM((width, width), BF),
            pltpu.VMEM((8, width), F32),
            pltpu.VMEM((slots, width), BF),
            pltpu.VMEM((3, slots, third), BF),
            pltpu.VMEM((slots, third), BF),
            pltpu.VMEM((2, HALF, third), BF),
            pltpu.VMEM((2, 2, HALF, 2 * third), BF),
            pltpu.VMEM((2 * heads, SLOT, SLOT), BF),
            pltpu.VMEM((slots, width), BF),
            pltpu.VMEM((slots, width), BF),
            pltpu.VMEM((2, HALF, width), F32),
            pltpu.VMEM((2, HALF, width), F32),
            pltpu.VMEM((HALF, width), F32),
            pltpu.VMEM((slots, third), BF),
            pltpu.VMEM((heads, slots, third), BF),
            pltpu.VMEM((heads, third, width), BF),
            pltpu.VMEM((SLOT, SLOT), BF),
            pltpu.VMEM((slots, width), F32),
            pltpu.VMEM((HALF, width), F32),
            pltpu.VMEM((7, 8, width), F32),
            pltpu.VMEM((heads, 8, third), F32),
            pltpu.VMEM((HALF, width), BF),
            pltpu.VMEM((2, 3, HALF, width), BF),
            pltpu.VMEM((2, 3, HALF, width), BF),
            pltpu.VMEM((2, 3, HALF, width), BF),
            pltpu.VMEM((grad_rows, width), BF),
            pltpu.VMEM((grad_rows, width), BF),
            pltpu.VMEM((extra, grad_rows // 4 if levels > 3 else 16, width), BF),
            pltpu.VMEM((8, width), F32),
            pltpu.VMEM((16, 128), F32),
            pltpu.VMEM((slots, width), BF),
            pltpu.VMEM((slots, width), BF),
            pltpu.VMEM((8, width), F32),
            pltpu.VMEM((levels, 8, width), F32),
            pltpu.VMEM((16, 128), F32),
            pltpu.VMEM((levels, 16, 128), F32),
            dma((16,)),
            dma((3,)),
            dma((3,)),
            dma((2, 2)),
            dma((2, 2)),
            dma((2, 3)),
            dma((2, 3)),
            dma((2, 3)),
            dma((2, 3)),
            dma((2, 4)),
            dma((2, 4)),
            dma((8, 5 + extra)),
            dma((8, 5 + extra)),
            dma((2 + 2 * levels,)),
            dma((2 + 2 * levels,)),
        ]
        + [pltpu.VMEM((size >> min(i + 1, 2), width), BF) for _, size, _ in dp_units(width, third) for i in range(3)]
        + [pltpu.VMEM((HALF, width), BF)] * 8,
        compiler_params=pltpu.CompilerParams(
            collective_id=0, has_side_effects=True, vmem_limit_bytes=67043328
        ),
    )(*operands)


def body(
    n_dp,
    tokens,
    cotangent,
    image_group,
    image_length,
    first_gain,
    first_shift,
    qkv_weight,
    qv_bias,
    out_weight,
    out_bias,
    second_gain,
    second_shift,
    up_weight,
    up_bias,
    down_weight,
    down_bias,
):
    third = out_weight.shape[0]
    width = tokens.shape[1]
    block, ingrad, grads, small = call_layer(
        n_dp,
        image_group,
        image_length,
        tokens,
        cotangent,
        jnp.transpose(qkv_weight, (1, 2, 0)),
        out_weight,
        up_weight,
        down_weight,
        first_gain,
        first_shift,
        out_bias,
        second_gain,
        second_shift,
        down_bias,
        up_bias,
        qv_bias,
    )
    outs = call_unpack(block, ingrad, grads, small, third)
    block_out, input_grad, down_grad, up_grad, out_grad, qkv_grad = outs[:6]
    g1, b1, g2, b2, out_bias_grad, down_bias_grad, up_bias_grad, qv_bias_grad = outs[6:]
    return (
        block_out,
        input_grad,
        g1,
        b1,
        jnp.transpose(qkv_grad.reshape(3, third, width), (2, 0, 1)),
        qv_bias_grad,
        out_grad,
        out_bias_grad,
        g2,
        b2,
        up_grad,
        up_bias_grad,
        down_grad,
        down_bias_grad,
    )


def solution(mesh):
    in_specs = (
        P("dp", None),
        P("dp", None),
        P(),
        P(),
        P(),
        P(),
        P(None, None, "tensor"),
        P(None, "tensor"),
        P("tensor", None),
        P(),
        P(),
        P(),
        P(None, "tensor"),
        P("tensor"),
        P("tensor", None),
        P(),
    )
    out_specs = (
        P("dp", None),
        P("dp", None),
        P(),
        P(),
        P(None, None, "tensor"),
        P(None, "tensor"),
        P("tensor", None),
        P(),
        P(),
        P(),
        P(None, "tensor"),
        P("tensor"),
        P("tensor", None),
        P(),
    )
    return jax.shard_map(
        functools.partial(body, mesh.shape["dp"]), mesh=mesh, in_specs=in_specs, out_specs=out_specs, check_vma=False
    )
```

```python
import functools

import jax
import jax.numpy as jnp
from jax import lax
from jax.experimental import pallas as pl
from jax.experimental.pallas import tpu as pltpu
from jax.sharding import PartitionSpec as P

HD = 64
RES_SMALL = 197
RES_LARGE = 577
SMALL_START = RES_SMALL // 16 * 16
LARGE_START = RES_LARGE // 16 * 16
SLOT = 608
HALF = 304
EPS = 1e-06
MASKED = -1e30
BF = jnp.bfloat16
F32 = jnp.float32
MESH = pl.DeviceIdType.MESH


def dot_nn(a, b):
    return lax.dot_general(a, b, (((1,), (0,)), ((), ())), preferred_element_type=F32)


def dot_nt(a, b):
    return lax.dot_general(a, b, (((1,), (1,)), ((), ())), preferred_element_type=F32)


def dot_tn(a, b):
    return lax.dot_general(a, b, (((0,), (0,)), ((), ())), preferred_element_type=F32)


def normalize(x):
    mean = jnp.mean(x, axis=-1, keepdims=True)
    centered = x - mean
    var = jnp.mean(centered * centered, axis=-1, keepdims=True)
    scale = lax.rsqrt(var + EPS)
    return centered * scale, scale


def norm_back(u, xn, scale):
    return scale * (
        u
        - jnp.mean(u, axis=-1, keepdims=True)
        - xn * jnp.mean(u * xn, axis=-1, keepdims=True)
    )


def fold8(x):
    return jnp.sum(x.reshape(x.shape[0] // 8, 8, x.shape[1]), axis=0)


def flip(index, stride):
    return index + stride - 2 * stride * ((index // stride) % 2)


def row_loop(count, size, unroll, step, init):
    block = size * unroll

    def several(i, carry):
        for j in range(unroll):
            carry = step(pl.multiple_of(i * block + j * size, 16), carry)
        return carry

    carry = lax.fori_loop(0, count // block, several, init)
    for off in range(count // block * block, count, size):
        carry = step(off, carry)
    return carry


FIRST, SECOND = (0, 1, 2), (1, 0, 2)
ORDERS = (FIRST, SECOND, FIRST, FIRST, FIRST, FIRST, FIRST, SECOND)
PLAN = {
    "back0": ((0, 0), (1, 0)),
    "head010": ((2, 0), (0, 1)),
    "back1": (("early", 0),),
    "head021": ((2, 1), (3, 0)),
    "out": (("early", 1), (1, 1), (0, 2)),
    "head101": (("early", 2),),
    "head110": ((4, 0), (3, 1), (2, 2)),
    "head111": (("early", 3),),
    "head120": ((5, 0),),
    "head121": ((0, 3), ("early", 4)),
    "heads": ((1, 2), (4, 1), (6, 0)),
    "block": ((3, 2), (2, 3), (0, 4), (5, 1), (4, 2)),
    "grad0": ((1, 3), (7, 0), (5, 2), (6, 1), (2, 4), (3, 3), (7, 1)),
    "grad1": (
        (6, 2),
        (4, 3),
        ("late", 1),
        (7, 2),
        (3, 4),
        (1, 4),
        (5, 3),
        (4, 4),
        ("late", 2),
        (7, 3),
        (6, 3),
        ("late", 3),
        (5, 4),
        ("late", 4),
        (7, 4),
        (6, 4),
    ),
}


def dp_units(width, third):
    units, start = [], 0
    for size, order in zip((width // 2,) * 4 + (third,) * 4, ORDERS, strict=True):
        units.append((start, size, order))
        start += size
    return units


def layer_kernel(
    n_dp,
    group,
    lengths,
    tok_h,
    cot_h,
    wqkv_h,
    wout_h,
    wup_h,
    wdown_h,
    g1,
    b1,
    ob,
    g2,
    b2,
    db,
    ub,
    qvb,
    block_h,
    ingrad_h,
    grads_h,
    small_o,
    tok,
    cot,
    wqkv,
    wout,
    wup,
    wdown,
    vec,
    normed,
    qkv,
    att,
    attc,
    attf,
    probs,
    hidden,
    pregrad,
    middle,
    midgrad,
    keep,
    agrad,
    dhead,
    wstack,
    sgrad,
    slope,
    tmp_a,
    acc,
    acch,
    csend,
    crecv,
    ysend,
    yrecv,
    gbuf,
    obuf,
    rx,
    early,
    late,
    block,
    ingrad,
    early_c,
    early_r,
    late_c,
    late_r,
    l_sem,
    w_send,
    w_recv,
    a_send,
    a_recv,
    c_send,
    c_recv,
    y_send,
    y_recv,
    g_send,
    g_recv,
    d_send,
    d_recv,
    s_send,
    s_recv,
    ready,
    *more,
):
    rs, normed2, mg = more[:24], (more[24:26], more[26:28]), (more[28:30], more[30:32])
    levels = n_dp.bit_length() - 1
    d = lax.axis_index("dp")
    t = lax.axis_index("tensor")
    core = t % 2
    side = t // 2
    core_peer = (d, flip(t, 1))
    y_peer = (d, flip(t, 2))
    rows, width = tok_h.shape
    third = wout_h.shape[0]
    heads = third // HD

    def dp_peer(level):
        return (flip(d, 2**level), t)

    def local(i, src, dst):
        return pltpu.make_async_copy(src, dst, l_sem.at[i])

    my_quarter = pl.ds(pl.multiple_of(t * third, 16), third)
    its_quarter = pl.ds(pl.multiple_of(flip(t, 2) * third, 16), third)
    loads = [
        local(0, tok_h, tok.at[0:rows]),
        local(1, wqkv_h, wqkv),
        local(2, wout_h, wout.at[my_quarter]),
        local(3, cot_h, hidden.at[0:rows]),
        local(4, wup_h, wup),
        local(5, wdown_h, wdown),
    ]
    for copy in loads:
        copy.start()
    bar = pltpu.get_barrier_semaphore()
    peers = [core_peer, y_peer] + [dp_peer(i) for i in range(levels)]
    for peer in peers:
        pl.semaphore_signal(bar, inc=1, device_id=peer, device_id_type=MESH)

    def look(i, found):
        count, first, second = found
        here = group[i] == d
        first = jnp.where(here & (count == 0), lengths[i], first)
        second = jnp.where(here & (count == 1), lengths[i], second)
        return count + here.astype(jnp.int32), first, second

    zero = jnp.int32(0)
    _, first_len, second_len = lax.fori_loop(0, group.shape[0], look, (zero, zero, zero))
    first_small = first_len == RES_SMALL
    second_skip = jnp.where(first_small, RES_SMALL % 16, RES_LARGE % 16)

    def group_rows(ref, s, off, size):
        small = ref[pl.ds(pl.multiple_of(s * SMALL_START + off, 16), size), :].astype(F32)
        large = ref[pl.ds(pl.multiple_of(s * LARGE_START + off, 16), size), :].astype(F32)
        return jnp.where(first_small, small, large)

    def inside(s, index):
        low = s * second_skip
        return (index >= low) & (index < low + jnp.where(s == 0, first_len, second_len))

    for i, ref in enumerate((g1, b1, ob, g2, b2, db, ub)):
        vec[i : i + 1, :] = ref[...][None, :]
    gain1, shift1, bias_out, gain2, shift2, bias_down, bias_up = (vec.at[i : i + 1] for i in range(7))
    acc[...] = jnp.zeros_like(acc)
    acch[...] = jnp.zeros_like(acch)
    tok[rows:, :] = jnp.zeros((tok.shape[0] - rows, width), BF)

    own, other = 0, HALF
    half_start = (core * HALF, (1 - core) * HALF)
    zero8 = jnp.zeros((8, width), F32)

    def slot_rows(s, off, size):
        return pl.ds(pl.multiple_of(s * SLOT + off, 16), size)

    def remote(src, dst, send, recv, peer):
        return pltpu.make_async_remote_copy(
            src_ref=src, dst_ref=dst, send_sem=send, recv_sem=recv, device_id=peer, device_id_type=MESH
        )

    def c_copy(s, k):
        return remote(csend, crecv.at[s, k], c_send.at[s, k], c_recv.at[s, k], core_peer)

    def y_copy(s, k):
        return remote(ysend.at[s, k], yrecv.at[s, k], y_send.at[s, k], y_recv.at[s, k], y_peer)

    def half_copy(refs, s, k):
        return remote(refs[s][0], refs[s][1], g_send.at[s, k], g_recv.at[s, k], core_peer)

    def gather_copy(ref, s, k):
        region = slot_rows(s, half_start[0], HALF)
        return remote(ref.at[region], ref.at[region], g_send.at[s, k], g_recv.at[s, k], core_peer)

    def begin(s, k, part):
        csend[...] = part(other).astype(BF)
        c_copy(s, k).start()
        keep[...] = part(own)

    def end(s, k):
        c_copy(s, k).wait()

        def add(off, carry):
            r = pl.ds(off, 16)
            ysend[s, k, r, :] = (keep[r, :] + crecv[s, k, r, :].astype(F32)).astype(BF)
            return carry

        row_loop(HALF, 16, 6, add, 0)
        y_copy(s, k).start()

    def total(s, k, r):
        return ysend[s, k, r, :].astype(F32) + yrecv[s, k, r, :].astype(F32)

    units = dp_units(width, third)

    def bit(level):
        return (d // 2**level) % 2

    def base(u, depth):
        row0, size, order = units[u]
        for i in range(depth):
            row0 = row0 + bit(order[i]) * (size >> (i + 1))
        return row0

    def region(u, depth):
        return pl.ds(pl.multiple_of(base(u, depth), 16), units[u][1] >> depth)

    def dp_rs(u, i):
        _, size, order = units[u]
        part = size >> (i + 1)
        src = pl.ds(pl.multiple_of(base(u, i) + (1 - bit(order[i])) * part, 16), part)
        return remote(gbuf.at[src], rs[3 * u + i], d_send.at[u, i], d_recv.at[u, i], dp_peer(order[i]))

    def dp_swap(u):
        return remote(gbuf.at[region(u, 2)], rs[3 * u + 2], d_send.at[u, 2], d_recv.at[u, 2], dp_peer(units[u][2][2]))

    def dp_ag(u, i):
        mine = obuf.at[region(u, i + 1)]
        return remote(mine, mine, d_send.at[u, 3 + i], d_recv.at[u, 3 + i], dp_peer(units[u][2][i]))

    def dp_add(u, i, out):
        start = base(u, min(i + 1, 2))

        def add(off, carry):
            r = pl.ds(pl.multiple_of(start + off, 16), 16)
            out[r, :] = (gbuf[r, :].astype(F32) + rs[3 * u + i][pl.ds(off, 16), :].astype(F32)).astype(BF)
            return carry

        row_loop(units[u][1] >> min(i + 1, 2), 16, 3, add, 0)

    def dp_further(u):
        size, mine = units[u][1] >> 2, region(u, 2)
        for e in range(levels - 3):
            peer = dp_peer(3 + e)
            pl.semaphore_signal(ready.at[e], inc=1, device_id=peer, device_id_type=MESH)
            pl.semaphore_wait(ready.at[e], 1)
            copy = remote(obuf.at[mine], rx.at[0:size], d_send.at[u, 5 + e], d_recv.at[u, 5 + e], peer)
            copy.start()
            copy.wait()
            obuf[mine, :] = (obuf[mine, :].astype(F32) + rx[0:size, :].astype(F32)).astype(BF)

    def dp_out(u):
        row0, size, _ = units[u]
        return local(6 + u, obuf.at[row0 : row0 + size], grads_h.at[row0 : row0 + size])

    def advance(u, k):
        if k == 0:
            dp_rs(u, 0).wait()
            dp_add(u, 0, gbuf)
            dp_rs(u, 1).start()
        elif k == 1:
            dp_rs(u, 1).wait()
            dp_add(u, 1, gbuf)
            dp_swap(u).start()
        elif k == 2:
            dp_swap(u).wait()
            dp_add(u, 2, obuf)
            dp_further(u)
            dp_ag(u, 1).start()
        elif k == 3:
            dp_ag(u, 1).wait()
            dp_ag(u, 0).start()
        else:
            dp_ag(u, 0).wait()
            dp_out(u).start()

    def serve(place):
        for u, k in PLAN.get(place, ()):
            if u == "early":
                early_step(k)
            elif u == "late":
                late_step(k)
            else:
                advance(u, k)

    def exchange(buf, landing, sem, peer):
        return remote(buf, landing, s_send.at[sem], s_recv.at[sem], peer)

    def early_step(k):
        if k == 0:
            early[...] = jnp.zeros_like(early)
            for i in range(4):
                early[i : i + 1, :] = jnp.sum(acc[2 + i], axis=0, keepdims=True)
            exchange(early, early_c, 0, core_peer).start()
            return
        landing = early_c if k == 1 else early_r.at[k - 2]
        exchange(early, landing, k - 1, core_peer if k == 1 else dp_peer(k - 2)).wait()
        early[...] = early[...] + landing[...]
        if k == 1:
            early[4:5, :] = jnp.sum(acc[6], axis=0, keepdims=True)
        if k <= levels:
            exchange(early, early_r.at[k - 1], k, dp_peer(k - 1)).start()

    tiles = width // 128

    def late_step(k):
        first = 1 + levels
        if k == 0:
            late[...] = jnp.zeros_like(late)
            for i in range(2):
                row = jnp.sum(acc[i], axis=0, keepdims=True)
                for j in range(tiles):
                    late[i * tiles + j : i * tiles + j + 1, :] = row[:, j * 128 : (j + 1) * 128]
            exchange(late, late_c, first, core_peer).start()
            return
        landing = late_c if k == 1 else late_r.at[k - 2]
        exchange(late, landing, first + k - 1, core_peer if k == 1 else dp_peer(k - 2)).wait()
        late[...] = late[...] + landing[...]
        if k == 1:
            for h in range(heads):
                row = jnp.sum(acch[h], axis=0, keepdims=True)
                late[2 * tiles + h : 2 * tiles + h + 1, 0:HD] = row[:, 0:HD]
                late[2 * tiles + h : 2 * tiles + h + 1, HD : 2 * HD] = row[:, 2 * HD : 3 * HD]
        if k <= levels:
            exchange(late, late_r.at[k - 1], first + k, dp_peer(k - 1)).start()

    def norm_rows(s):
        for half, start in enumerate(half_start):

            def step(off, carry):
                xn, _ = normalize(group_rows(tok, s, start + off, 16))
                normed[slot_rows(s, half * HALF + off, 16), :] = (xn * gain1[...] + shift1[...]).astype(BF)
                return carry

            row_loop(HALF, 16, 6, step, 0)

    def mask_rows(s):
        for half, start in enumerate(half_start):

            def step(off, carry):
                ok = inside(s, lax.broadcasted_iota(jnp.int32, (16, 1), 0) + (start + off))
                value = group_rows(hidden, s, start + off, 16)
                cot[slot_rows(s, half * HALF + off, 16), :] = jnp.where(ok, value, 0.0).astype(BF)
                return carry

            row_loop(HALF, 16, 6, step, 0)

    loads[0].wait()
    norm_rows(0)
    pl.semaphore_wait(bar, len(peers))
    loads[2].wait()
    w_own = [
        remote(wout.at[my_quarter], wout.at[my_quarter], w_send.at[0], w_recv.at[0], core_peer),
        remote(wout.at[my_quarter], wout.at[my_quarter], w_send.at[1], w_recv.at[1], y_peer),
    ]
    w_pass = remote(wout.at[its_quarter], wout.at[its_quarter], w_send.at[2], w_recv.at[2], core_peer)
    for copy in w_own:
        copy.start()
    loads[1].wait()
    norm_rows(1)
    for h in range(heads):
        for j in range(3):
            wstack[h, j * HD : (j + 1) * HD, :] = wqkv[j, h * HD : (h + 1) * HD, :]

    def a_swap(s):
        return remote(att.at[slot_rows(s, other, HALF)], attc.at[s], a_send.at[s, 0], a_recv.at[s, 0], core_peer)

    def a_copy(s):
        return remote(attf.at[s, side], attf.at[s, side], a_send.at[s, 1], a_recv.at[s, 1], y_peer)

    def project(s):
        def half(i, carry):
            r = slot_rows(s, i * HALF, HALF)
            x = normed[r, :]
            qkv[0, r, :] = (dot_nt(x, wqkv[0]) + qvb[0:1, :]).astype(BF)
            qkv[1, r, :] = dot_nt(x, wqkv[1]).astype(BF)
            qkv[2, r, :] = (dot_nt(x, wqkv[2]) + qvb[1:2, :]).astype(BF)
            return carry

        lax.fori_loop(0, 2, half, 0)

    def attend(s):
        whole = slot_rows(s, 0, SLOT)
        key = lax.broadcasted_iota(jnp.int32, (1, SLOT), 1)
        key = key + jnp.where(key < HALF, half_start[0], half_start[1] - HALF)
        key_bias = jnp.where(inside(s, key), 0.0, MASKED)

        def half(i, carry):
            r = slot_rows(s, i * HALF, HALF)
            for h in range(heads):
                lanes = slice(h * HD, (h + 1) * HD)
                q = (qkv[0, r, lanes] * HD**-0.5).astype(BF)
                scores = dot_nt(q, qkv[1, whole, lanes]) + key_bias
                exps = jnp.exp(scores - jnp.max(scores, axis=-1, keepdims=True))
                weights = (exps * (1.0 / jnp.sum(exps, axis=-1, keepdims=True))).astype(BF)
                probs[s * heads + h, pl.ds(pl.multiple_of(i * HALF, 16), HALF), :] = weights
                att[r, lanes] = dot_nn(weights, qkv[2, whole, lanes]).astype(BF)
            return carry

        lax.fori_loop(0, 2, half, 0)
        a_swap(s).start()

    def join(s):
        a_swap(s).wait()
        mine, its = att[slot_rows(s, own, HALF), :], attc[s]
        left = jnp.where(core == 0, mine, its)
        right = jnp.where(core == 0, its, mine)
        attf[s, side] = jnp.concatenate([left, right], axis=1)
        a_copy(s).start()

    project(0)
    attend(0)
    project(1)
    join(0)
    attend(1)
    w_own[1].wait()
    w_pass.start()
    loads[3].wait()
    mask_rows(0)
    join(1)
    mask_rows(1)
    w_own[0].wait()
    w_pass.wait()
    loads[4].wait()
    loads[5].wait()

    def second_norm(s):
        a_copy(s).wait()
        tmp_a[...] = dot_nn(jnp.concatenate([attf[s, 0], attf[s, 1]], axis=1), wout[...])

        def step(off, carry):
            r = pl.ds(off, 16)
            m = tmp_a[r, :] + group_rows(tok, s, half_start[0] + off, 16) + bias_out[...]
            middle[s, r, :] = m
            xn, _ = normalize(m)
            normed2[s][0][r, :] = (xn * gain2[...] + shift2[...]).astype(BF)
            return carry

        row_loop(HALF, 16, 6, step, 0)
        half_copy(normed2, s, 0).start()

    def up_half(s, half):
        tmp_a[...] = dot_nn(normed2[s][half][...], wup[...])

        def step(off, carry):
            g = slot_rows(s, half * HALF + off, 16)
            x = tmp_a[pl.ds(off, 16), :] + bias_up[...]
            phi = 0.5 + 0.5 * lax.erf(x * 0.7071067811865476)
            hidden[g, :] = (x * phi).astype(BF)
            slope[g, :] = phi + x * (jnp.exp(x * x * -0.5) * 0.3989422804014327)
            return carry

        row_loop(HALF, 16, 2, step, 0)

    def back_half(s, half):
        tmp_a[...] = dot_nt(cot[slot_rows(s, half * HALF, HALF), :], wdown[...])

        def step(off, sums):
            g = slot_rows(s, half * HALF + off, 16)
            low = (tmp_a[pl.ds(off, 16), :] * slope[g, :]).astype(BF)
            pregrad[g, :] = low
            return sums + fold8(low.astype(F32))

        acc[6] += row_loop(HALF, 16, 6, step, zero8)

    def unit_grad(u, left, right):
        row0, size, _ = units[u]
        gbuf[row0 : row0 + size, :] = dot_tn(left, right[...]).astype(BF)
        dp_rs(u, 0).start()

    def norm_columns(columns):
        return jnp.concatenate([ref[:, columns] for refs in normed2 for ref in refs], axis=0)

    lower, upper = slice(0, width // 2), slice(width // 2, width)
    def norm_part(s):
        begin(s, 0, lambda off: dot_nt(pregrad[slot_rows(s, off, HALF), :], wup[...]))

    def out_part(s):
        begin(s, 1, lambda off: dot_nn(hidden[slot_rows(s, off, HALF), :], wdown[...]))

    second_norm(0)
    up_half(0, 0)
    half_copy(normed2, 0, 0).wait()
    up_half(0, 1)
    back_half(0, 1)
    back_half(0, 0)
    norm_part(0)
    second_norm(1)
    end(0, 0)
    up_half(1, 0)
    half_copy(normed2, 1, 0).wait()
    up_half(1, 1)
    unit_grad(0, hidden[:, lower], cot)
    unit_grad(1, hidden[:, upper], cot)
    back_half(1, 1)
    back_half(1, 0)
    norm_part(1)
    unit_grad(2, norm_columns(lower), pregrad)
    end(1, 0)
    out_part(0)
    unit_grad(3, norm_columns(upper), pregrad)
    end(0, 1)
    out_part(1)

    def second_back(s):
        y_copy(s, 0).wait()

        def step(off, sums):
            r = pl.ds(off, 16)
            g = slot_rows(s, own + off, 16)
            n = total(s, 0, r)
            xn, scale = normalize(middle[s, r, :])
            og = cot[g, :].astype(F32)
            m = og + norm_back(n * gain2[...], xn, scale)
            midgrad[s, r, :] = m
            mg[s][0][r, :] = m.astype(BF)
            return tuple(a + fold8(b) for a, b in zip(sums, (n * xn, n, m, og), strict=True))

        sums = row_loop(HALF, 16, 3, step, (zero8,) * 4)
        for i in range(4):
            acc[2 + i] += sums[i]
        half_copy(mg, s, 1).start()

    def head_back(s, h):
        whole = slot_rows(s, 0, SLOT)
        lanes = slice(h * HD, (h + 1) * HD)
        keys, values = qkv[1, whole, lanes], qkv[2, whole, lanes]
        for c in (0, 1):
            r = slot_rows(s, c * HALF, HALF)
            part = slice(c * HALF, (c + 1) * HALF)
            p = probs[s * heads + h, part, :].astype(F32)
            prob_grad = dot_nt(agrad[r, lanes], values)
            inner = jnp.sum(p * prob_grad, axis=-1, keepdims=True)
            sgrad[part, :] = (p * (prob_grad - inner)).astype(BF)
            dhead[h, r, 0:HD] = (dot_nn(sgrad[part, :], keys) * HD**-0.5).astype(BF)
            serve(f"head{s}{h}{c}")
        dhead[h, whole, HD : 2 * HD] = (dot_tn(sgrad[...], qkv[0, whole, lanes]) * HD**-0.5).astype(BF)
        dhead[h, whole, 2 * HD : 3 * HD] = dot_tn(probs[s * heads + h], agrad[whole, lanes]).astype(BF)
        acch[h] += fold8(dhead[h, whole, :].astype(F32))

    def attended_grad(s):
        half_copy(mg, s, 1).wait()
        agrad[slot_rows(s, 0, SLOT), :] = dot_nt(
            jnp.concatenate([mg[s][0][...], mg[s][1][...]], axis=0), wout[my_quarter, :]
        ).astype(BF)

    def projected(s):
        def part(off):
            r = slot_rows(s, off, HALF)
            return sum(dot_nn(dhead[h, r, :], wstack[h]) for h in range(heads))

        begin(s, 2, part)

    second_back(0)
    end(1, 1)
    serve("back0")
    attended_grad(0)
    for h in range(heads - 1):
        head_back(0, h)
    second_back(1)
    serve("back1")
    head_back(0, heads - 1)
    projected(0)
    attended_grad(1)
    end(0, 2)
    all_mg = jnp.concatenate([ref[...] for refs in mg for ref in refs], axis=0)
    gbuf[2 * width : 2 * width + third, :] = dot_tn(att[...], all_mg).astype(BF)
    dp_rs(4, 0).start()
    serve("out")
    for h in range(heads):
        head_back(1, h)
        if h == heads - 1:
            projected(1)
        unit_grad(5 + h, dhead[h], normed)
    serve("heads")
    end(1, 2)

    def finish_block(s):
        y_copy(s, 1).wait()

        def step(off, carry):
            r = pl.ds(off, 16)
            block[slot_rows(s, half_start[0] + off, 16), :] = (middle[s, r, :] + total(s, 1, r) + bias_down[...]).astype(BF)
            return carry

        row_loop(HALF, 16, 6, step, 0)
        gather_copy(block, s, 2).start()

    def finish_grad(s):
        y_copy(s, 2).wait()

        def step(off, sums):
            r = pl.ds(off, 16)
            n = total(s, 2, r)
            xn, scale = normalize(group_rows(tok, s, half_start[0] + off, 16))
            ingrad[slot_rows(s, half_start[0] + off, 16), :] = (midgrad[s, r, :] + norm_back(n * gain1[...], xn, scale)).astype(BF)
            return tuple(a + fold8(b) for a, b in zip(sums, (n * xn, n), strict=True))

        sums = row_loop(HALF, 16, 4, step, (zero8,) * 2)
        for i in range(2):
            acc[i] += sums[i]
        gather_copy(ingrad, s, 3).start()

    def assemble(ref):
        def step(off, carry):
            index = lax.broadcasted_iota(jnp.int32, (16, 1), 0) + off

            def two_from(start):
                source = jnp.clip(off - start, 0, SLOT - 16) + SLOT
                return ref[pl.ds(pl.multiple_of(source, 16), 16), :].astype(F32)

            two = jnp.where(first_small, two_from(SMALL_START), two_from(LARGE_START))
            low = jnp.minimum(off, SLOT - 16)
            one = ref[pl.ds(pl.multiple_of(low, 16), 16), :].astype(F32)
            both = jnp.where(index < first_len, one, two)
            ref[pl.ds(off, 16), :] = jnp.where(index < first_len + second_len, both, 0.0).astype(BF)
            return carry

        row_loop(rows, 16, 1, step, 0)

    finish_block(0)
    finish_block(1)
    for s in (0, 1):
        gather_copy(block, s, 2).wait()
    assemble(block)
    out_block = local(14, block.at[0:rows], block_h)
    out_block.start()
    serve("block")
    finish_grad(0)
    serve("grad0")
    finish_grad(1)
    late_step(0)
    for s in (0, 1):
        gather_copy(ingrad, s, 3).wait()
    assemble(ingrad)
    out_grad = local(15, ingrad.at[0:rows], ingrad_h)
    out_grad.start()
    serve("grad1")
    for k in range(5, levels + 2):
        early_step(k)
        late_step(k)

    small_o[...] = jnp.zeros_like(small_o)
    for i in range(2):
        for j in range(tiles):
            small_o[i : i + 1, j * 128 : (j + 1) * 128] = late[i * tiles + j : i * tiles + j + 1, :]
    small_o[2:6, :] = early[0:4, :]
    small_o[8:9, :] = early[4:5, :]
    for h in range(heads):
        row = late[2 * tiles + h : 2 * tiles + h + 1, :]
        small_o[9:10, h * HD : (h + 1) * HD] = row[:, 0:HD]
        small_o[10:11, h * HD : (h + 1) * HD] = row[:, HD : 2 * HD]
    out_block.wait()
    out_grad.wait()
    for u in range(len(units)):
        dp_out(u).wait()


def unpack_kernel(block, ingrad, down, up, out, qkv0, qkv1, qkv2, small, *outs):
    outs[0][...] = block[...]
    outs[1][...] = ingrad[...].astype(F32)
    outs[2][...] = down[...].astype(F32)
    outs[3][...] = up[...].astype(F32)
    outs[4][...] = out[...].astype(F32)
    for i, qkv in enumerate((qkv0, qkv1, qkv2)):
        rows = qkv.shape[0]
        outs[5][i * rows : (i + 1) * rows, :] = qkv[...].astype(F32)

    @pl.when(pl.program_id(0) == 0)
    def _():
        for i, row in enumerate((0, 1, 2, 3, 4, 5, 8)):
            outs[6 + i][...] = small[row]
        outs[13][...] = small[9:11, 0 : outs[13].shape[1]]


def call_unpack(block, ingrad, grads, small, third):
    rows, width = block.shape
    steps = 6
    row_block = -(-rows // (16 * steps)) * 16

    def part(size, start):
        return pl.BlockSpec((size, width), lambda i: (start // size + i, 0))

    def whole(shape):
        return pl.BlockSpec(shape, lambda i: (0,) * len(shape))

    big, mid, low = width // steps, 3 * third // steps, third // steps
    piece = mid // 3
    per_head = HD // piece

    def qkv_part(b, i):
        m = 3 * i + b
        kind, rest = m // (third // piece), m % (third // piece)
        head, low_part = rest // per_head, rest % per_head
        return (2 * width + third) // piece + (head * 3 + kind) * per_head + low_part, 0

    shapes = [
        ((rows, width), BF, part(row_block, 0)),
        ((rows, width), F32, part(row_block, 0)),
        ((width, width), F32, part(big, 0)),
        ((width, width), F32, part(big, 0)),
        ((third, width), F32, part(low, 0)),
        ((3 * third, width), F32, part(mid, 0)),
    ]
    shapes += [((width,), F32, whole((width,)))] * 7 + [((2, third), F32, whole((2, third)))]
    return pl.pallas_call(
        unpack_kernel,
        grid=(steps,),
        out_shape=[jax.ShapeDtypeStruct(shape, kind) for shape, kind, _ in shapes],
        in_specs=[
            part(row_block, 0),
            part(row_block, 0),
            part(big, 0),
            part(big, width),
            part(low, 2 * width),
            *(pl.BlockSpec((piece, width), functools.partial(qkv_part, b)) for b in range(3)),
            whole(small.shape),
        ],
        out_specs=[spec for _, _, spec in shapes],
    )(block, ingrad, grads, grads, grads, grads, grads, grads, small)


def call_layer(n_dp, *operands):
    rows, width = operands[2].shape
    third = operands[5].shape[0]
    heads = third // HD
    levels = n_dp.bit_length() - 1
    extra = max(levels - 3, 1)
    slots = 2 * SLOT
    grad_rows = 2 * width + 4 * third
    vmem = pl.BlockSpec(memory_space=pltpu.VMEM)
    smem = pl.BlockSpec(memory_space=pltpu.SMEM)
    hbm = pl.BlockSpec(memory_space=pl.ANY)
    dma = pltpu.SemaphoreType.DMA
    return pl.pallas_call(
        functools.partial(layer_kernel, n_dp),
        out_shape=(
            jax.ShapeDtypeStruct((rows, width), BF),
            jax.ShapeDtypeStruct((rows, width), BF),
            jax.ShapeDtypeStruct((grad_rows, width), BF),
            jax.ShapeDtypeStruct((16, width), F32),
        ),
        in_specs=[smem] * 2 + [hbm] * 6 + [vmem] * 8,
        out_specs=(hbm, hbm, hbm, vmem),
        scratch_shapes=[
            pltpu.VMEM((rows + 16, width), BF),
            pltpu.VMEM((slots, width), BF),
            pltpu.VMEM((3, third, width), BF),
            pltpu.VMEM((4 * third, width), BF),
            pltpu.VMEM((width, width), BF),
            pltpu.VMEM((width, width), BF),
            pltpu.VMEM((8, width), F32),
            pltpu.VMEM((slots, width), BF),
            pltpu.VMEM((3, slots, third), BF),
            pltpu.VMEM((slots, third), BF),
            pltpu.VMEM((2, HALF, third), BF),
            pltpu.VMEM((2, 2, HALF, 2 * third), BF),
            pltpu.VMEM((2 * heads, SLOT, SLOT), BF),
            pltpu.VMEM((slots, width), BF),
            pltpu.VMEM((slots, width), BF),
            pltpu.VMEM((2, HALF, width), F32),
            pltpu.VMEM((2, HALF, width), F32),
            pltpu.VMEM((HALF, width), F32),
            pltpu.VMEM((slots, third), BF),
            pltpu.VMEM((heads, slots, third), BF),
            pltpu.VMEM((heads, third, width), BF),
            pltpu.VMEM((SLOT, SLOT), BF),
            pltpu.VMEM((slots, width), F32),
            pltpu.VMEM((HALF, width), F32),
            pltpu.VMEM((7, 8, width), F32),
            pltpu.VMEM((heads, 8, third), F32),
            pltpu.VMEM((HALF, width), BF),
            pltpu.VMEM((2, 3, HALF, width), BF),
            pltpu.VMEM((2, 3, HALF, width), BF),
            pltpu.VMEM((2, 3, HALF, width), BF),
            pltpu.VMEM((grad_rows, width), BF),
            pltpu.VMEM((grad_rows, width), BF),
            pltpu.VMEM((width // 8 if levels > 3 else 16, width), BF),
            pltpu.VMEM((8, width), F32),
            pltpu.VMEM((16, 128), F32),
            pltpu.VMEM((slots, width), BF),
            pltpu.VMEM((slots, width), BF),
            pltpu.VMEM((8, width), F32),
            pltpu.VMEM((levels, 8, width), F32),
            pltpu.VMEM((16, 128), F32),
            pltpu.VMEM((levels, 16, 128), F32),
            dma((16,)),
            dma((3,)),
            dma((3,)),
            dma((2, 2)),
            dma((2, 2)),
            dma((2, 3)),
            dma((2, 3)),
            dma((2, 3)),
            dma((2, 3)),
            dma((2, 4)),
            dma((2, 4)),
            dma((8, 5 + extra)),
            dma((8, 5 + extra)),
            dma((2 + 2 * levels,)),
            dma((2 + 2 * levels,)),
            pltpu.SemaphoreType.REGULAR((extra,)),
        ]
        + [pltpu.VMEM((size >> min(i + 1, 2), width), BF) for _, size, _ in dp_units(width, third) for i in range(3)]
        + [pltpu.VMEM((HALF, width), BF)] * 8,
        compiler_params=pltpu.CompilerParams(
            collective_id=0, has_side_effects=True, vmem_limit_bytes=67043328
        ),
    )(*operands)


def body(
    n_dp,
    tokens,
    cotangent,
    image_group,
    image_length,
    first_gain,
    first_shift,
    qkv_weight,
    qv_bias,
    out_weight,
    out_bias,
    second_gain,
    second_shift,
    up_weight,
    up_bias,
    down_weight,
    down_bias,
):
    third = out_weight.shape[0]
    width = tokens.shape[1]
    block, ingrad, grads, small = call_layer(
        n_dp,
        image_group,
        image_length,
        tokens,
        cotangent,
        jnp.transpose(qkv_weight, (1, 2, 0)),
        out_weight,
        up_weight,
        down_weight,
        first_gain,
        first_shift,
        out_bias,
        second_gain,
        second_shift,
        down_bias,
        up_bias,
        qv_bias,
    )
    outs = call_unpack(block, ingrad, grads, small, third)
    block_out, input_grad, down_grad, up_grad, out_grad, qkv_grad = outs[:6]
    g1, b1, g2, b2, out_bias_grad, down_bias_grad, up_bias_grad, qv_bias_grad = outs[6:]
    return (
        block_out,
        input_grad,
        g1,
        b1,
        jnp.transpose(qkv_grad.reshape(3, third, width), (2, 0, 1)),
        qv_bias_grad,
        out_grad,
        out_bias_grad,
        g2,
        b2,
        up_grad,
        up_bias_grad,
        down_grad,
        down_bias_grad,
    )


def solution(mesh):
    in_specs = (
        P("dp", None),
        P("dp", None),
        P(),
        P(),
        P(),
        P(),
        P(None, None, "tensor"),
        P(None, "tensor"),
        P("tensor", None),
        P(),
        P(),
        P(),
        P(None, "tensor"),
        P("tensor"),
        P("tensor", None),
        P(),
    )
    out_specs = (
        P("dp", None),
        P("dp", None),
        P(),
        P(),
        P(None, None, "tensor"),
        P(None, "tensor"),
        P("tensor", None),
        P(),
        P(),
        P(),
        P(None, "tensor"),
        P("tensor"),
        P("tensor", None),
        P(),
    )
    return jax.shard_map(
        functools.partial(body, mesh.shape["dp"]), mesh=mesh, in_specs=in_specs, out_specs=out_specs, check_vma=False
    )
```

```python
import functools

import jax
import jax.numpy as jnp
from jax import lax
from jax.experimental import pallas as pl
from jax.experimental.pallas import tpu as pltpu
from jax.sharding import PartitionSpec as P

HD = 64
RES_SMALL = 197
RES_LARGE = 577
SMALL_START = RES_SMALL // 16 * 16
LARGE_START = RES_LARGE // 16 * 16
SLOT = 608
HALF = 304
EPS = 1e-06
MASKED = -1e30
BF = jnp.bfloat16
F32 = jnp.float32
MESH = pl.DeviceIdType.MESH


def dot_nn(a, b):
    return lax.dot_general(a, b, (((1,), (0,)), ((), ())), preferred_element_type=F32)


def dot_nt(a, b):
    return lax.dot_general(a, b, (((1,), (1,)), ((), ())), preferred_element_type=F32)


def dot_tn(a, b):
    return lax.dot_general(a, b, (((0,), (0,)), ((), ())), preferred_element_type=F32)


def normalize(x):
    mean = jnp.mean(x, axis=-1, keepdims=True)
    centered = x - mean
    var = jnp.mean(centered * centered, axis=-1, keepdims=True)
    scale = lax.rsqrt(var + EPS)
    return centered * scale, scale


def norm_back(u, xn, scale):
    return scale * (
        u
        - jnp.mean(u, axis=-1, keepdims=True)
        - xn * jnp.mean(u * xn, axis=-1, keepdims=True)
    )


def fold8(x):
    return jnp.sum(x.reshape(x.shape[0] // 8, 8, x.shape[1]), axis=0)


def flip(index, stride):
    return index + stride - 2 * stride * ((index // stride) % 2)


def row_loop(count, size, unroll, step, init):
    block = size * unroll

    def several(i, carry):
        for j in range(unroll):
            carry = step(pl.multiple_of(i * block + j * size, 16), carry)
        return carry

    carry = lax.fori_loop(0, count // block, several, init)
    for off in range(count // block * block, count, size):
        carry = step(off, carry)
    return carry


FIRST, SECOND = (0, 1, 2), (1, 0, 2)
ORDERS = (FIRST, SECOND, FIRST, FIRST, FIRST, FIRST, FIRST, SECOND)
PLAN = {
    "back0": ((0, 0), (1, 0)),
    "head001": ((2, 0),),
    "head010": ((0, 1),),
    "back1": (("early", 0),),
    "head011": ((3, 0),),
    "head020": ((2, 1),),
    "out": (("early", 1), (1, 1), (0, 2)),
    "head101": (("early", 2),),
    "head110": ((4, 0), (3, 1), (2, 2)),
    "head111": (("early", 3),),
    "head120": ((5, 0),),
    "head121": ((0, 3), ("early", 4)),
    "heads": ((1, 2), (4, 1), (6, 0)),
    "block": ((5, 1), (3, 2), (2, 3), (4, 2), (0, 4)),
    "grad0": ((7, 0), (1, 3), (6, 1), (5, 2), (3, 3), (7, 1), (2, 4)),
    "grad1": (
        (6, 2),
        (4, 3),
        ("late", 1),
        (7, 2),
        (3, 4),
        (1, 4),
        (5, 3),
        (4, 4),
        ("late", 2),
        (7, 3),
        (6, 3),
        ("late", 3),
        (5, 4),
        ("late", 4),
        (7, 4),
        (6, 4),
    ),
}


def dp_units(width, third):
    units, start = [], 0
    for size, order in zip((width // 2,) * 4 + (third,) * 4, ORDERS, strict=True):
        units.append((start, size, order))
        start += size
    return units


def layer_kernel(
    n_dp,
    group,
    lengths,
    tok_h,
    cot_h,
    wqkv_h,
    wout_h,
    wup_h,
    wdown_h,
    g1,
    b1,
    ob,
    g2,
    b2,
    db,
    ub,
    qvb,
    block_h,
    ingrad_h,
    grads_h,
    small_o,
    tok,
    cot,
    wqkv,
    wout,
    wup,
    wdown,
    vec,
    normed,
    qkv,
    att,
    attc,
    attf,
    probs,
    hidden,
    pregrad,
    middle,
    midgrad,
    keep,
    agrad,
    dhead,
    wstack,
    sgrad,
    slope,
    tmp_a,
    acc,
    acch,
    csend,
    crecv,
    ysend,
    yrecv,
    gbuf,
    obuf,
    rx,
    early,
    late,
    block,
    ingrad,
    early_c,
    early_r,
    late_c,
    late_r,
    l_sem,
    w_send,
    w_recv,
    a_send,
    a_recv,
    c_send,
    c_recv,
    y_send,
    y_recv,
    g_send,
    g_recv,
    d_send,
    d_recv,
    s_send,
    s_recv,
    ready,
    *more,
):
    rs, normed2, mg = more[:24], (more[24:26], more[26:28]), (more[28:30], more[30:32])
    levels = n_dp.bit_length() - 1
    d = lax.axis_index("dp")
    t = lax.axis_index("tensor")
    core = t % 2
    side = t // 2
    core_peer = (d, flip(t, 1))
    y_peer = (d, flip(t, 2))
    rows, width = tok_h.shape
    third = wout_h.shape[0]
    heads = third // HD

    def dp_peer(level):
        return (flip(d, 2**level), t)

    def local(i, src, dst):
        return pltpu.make_async_copy(src, dst, l_sem.at[i])

    my_quarter = pl.ds(pl.multiple_of(t * third, 16), third)
    its_quarter = pl.ds(pl.multiple_of(flip(t, 2) * third, 16), third)
    loads = [
        local(0, tok_h, tok.at[0:rows]),
        local(1, wqkv_h, wqkv),
        local(2, wout_h, wout.at[my_quarter]),
        local(3, cot_h, hidden.at[0:rows]),
        local(4, wup_h, wup),
        local(5, wdown_h, wdown),
    ]
    for copy in loads:
        copy.start()
    bar = pltpu.get_barrier_semaphore()
    peers = [core_peer, y_peer] + [dp_peer(i) for i in range(levels)]
    for peer in peers:
        pl.semaphore_signal(bar, inc=1, device_id=peer, device_id_type=MESH)

    def look(i, found):
        count, first, second = found
        here = group[i] == d
        first = jnp.where(here & (count == 0), lengths[i], first)
        second = jnp.where(here & (count == 1), lengths[i], second)
        return count + here.astype(jnp.int32), first, second

    zero = jnp.int32(0)
    _, first_len, second_len = lax.fori_loop(0, group.shape[0], look, (zero, zero, zero))
    first_small = first_len == RES_SMALL
    second_skip = jnp.where(first_small, RES_SMALL % 16, RES_LARGE % 16)

    def group_rows(ref, s, off, size):
        if s == 0:
            return ref[pl.ds(pl.multiple_of(off, 16), size), :].astype(F32)
        small = ref[pl.ds(pl.multiple_of(SMALL_START + off, 16), size), :].astype(F32)
        large = ref[pl.ds(pl.multiple_of(LARGE_START + off, 16), size), :].astype(F32)
        return jnp.where(first_small, small, large)

    def inside(s, index):
        low = s * second_skip
        return (index >= low) & (index < low + jnp.where(s == 0, first_len, second_len))

    for i, ref in enumerate((g1, b1, ob, g2, b2, db, ub)):
        vec[i : i + 1, :] = ref[...][None, :]
    gain1, shift1, bias_out, gain2, shift2, bias_down, bias_up = (vec.at[i : i + 1] for i in range(7))
    acc[...] = jnp.zeros_like(acc)
    acch[...] = jnp.zeros_like(acch)
    tok[rows:, :] = jnp.zeros((tok.shape[0] - rows, width), BF)

    own, other = 0, HALF
    half_start = (core * HALF, (1 - core) * HALF)
    zero8 = jnp.zeros((8, width), F32)

    def slot_rows(s, off, size):
        return pl.ds(pl.multiple_of(s * SLOT + off, 16), size)

    def remote(src, dst, send, recv, peer):
        return pltpu.make_async_remote_copy(
            src_ref=src, dst_ref=dst, send_sem=send, recv_sem=recv, device_id=peer, device_id_type=MESH
        )

    def c_copy(s, k):
        return remote(csend, crecv.at[s, k], c_send.at[s, k], c_recv.at[s, k], core_peer)

    def y_copy(s, k):
        return remote(ysend.at[s, k], yrecv.at[s, k], y_send.at[s, k], y_recv.at[s, k], y_peer)

    def half_copy(refs, s, k):
        return remote(refs[s][0], refs[s][1], g_send.at[s, k], g_recv.at[s, k], core_peer)

    def gather_copy(ref, s, k):
        region = slot_rows(s, half_start[0], HALF)
        return remote(ref.at[region], ref.at[region], g_send.at[s, k], g_recv.at[s, k], core_peer)

    def begin(s, k, part):
        csend[...] = part(other).astype(BF)
        c_copy(s, k).start()
        keep[...] = part(own)

    def end(s, k):
        c_copy(s, k).wait()

        def add(off, carry):
            r = pl.ds(off, 16)
            ysend[s, k, r, :] = (keep[r, :] + crecv[s, k, r, :].astype(F32)).astype(BF)
            return carry

        row_loop(HALF, 16, 6, add, 0)
        y_copy(s, k).start()

    def total(s, k, r):
        return ysend[s, k, r, :].astype(F32) + yrecv[s, k, r, :].astype(F32)

    units = dp_units(width, third)

    def bit(level):
        return (d // 2**level) % 2

    def base(u, depth):
        row0, size, order = units[u]
        for i in range(depth):
            row0 = row0 + bit(order[i]) * (size >> (i + 1))
        return row0

    def region(u, depth):
        return pl.ds(pl.multiple_of(base(u, depth), 16), units[u][1] >> depth)

    def dp_rs(u, i):
        _, size, order = units[u]
        part = size >> (i + 1)
        src = pl.ds(pl.multiple_of(base(u, i) + (1 - bit(order[i])) * part, 16), part)
        return remote(gbuf.at[src], rs[3 * u + i], d_send.at[u, i], d_recv.at[u, i], dp_peer(order[i]))

    def dp_swap(u):
        return remote(gbuf.at[region(u, 2)], rs[3 * u + 2], d_send.at[u, 2], d_recv.at[u, 2], dp_peer(units[u][2][2]))

    def dp_ag(u, i):
        mine = obuf.at[region(u, i + 1)]
        return remote(mine, mine, d_send.at[u, 3 + i], d_recv.at[u, 3 + i], dp_peer(units[u][2][i]))

    def dp_add(u, i, out):
        start = base(u, min(i + 1, 2))

        def add(off, carry):
            r = pl.ds(pl.multiple_of(start + off, 16), 16)
            out[r, :] = (gbuf[r, :].astype(F32) + rs[3 * u + i][pl.ds(off, 16), :].astype(F32)).astype(BF)
            return carry

        row_loop(units[u][1] >> min(i + 1, 2), 16, 3, add, 0)

    def dp_further(u):
        size, mine = units[u][1] >> 2, region(u, 2)
        for e in range(levels - 3):
            peer = dp_peer(3 + e)
            pl.semaphore_signal(ready.at[e], inc=1, device_id=peer, device_id_type=MESH)
            pl.semaphore_wait(ready.at[e], 1)
            copy = remote(obuf.at[mine], rx.at[0:size], d_send.at[u, 5 + e], d_recv.at[u, 5 + e], peer)
            copy.start()
            copy.wait()
            obuf[mine, :] = (obuf[mine, :].astype(F32) + rx[0:size, :].astype(F32)).astype(BF)

    def dp_out(u):
        row0, size, _ = units[u]
        return local(6 + u, obuf.at[row0 : row0 + size], grads_h.at[row0 : row0 + size])

    def advance(u, k):
        if k == 0:
            dp_rs(u, 0).wait()
            dp_add(u, 0, gbuf)
            dp_rs(u, 1).start()
        elif k == 1:
            dp_rs(u, 1).wait()
            dp_add(u, 1, gbuf)
            dp_swap(u).start()
        elif k == 2:
            dp_swap(u).wait()
            dp_add(u, 2, obuf)
            dp_further(u)
            dp_ag(u, 1).start()
        elif k == 3:
            dp_ag(u, 1).wait()
            dp_ag(u, 0).start()
        else:
            dp_ag(u, 0).wait()
            dp_out(u).start()

    def serve(place):
        for u, k in PLAN.get(place, ()):
            if u == "early":
                early_step(k)
            elif u == "late":
                late_step(k)
            else:
                advance(u, k)

    def exchange(buf, landing, sem, peer):
        return remote(buf, landing, s_send.at[sem], s_recv.at[sem], peer)

    def early_step(k):
        if k == 0:
            early[...] = jnp.zeros_like(early)
            for i in range(4):
                early[i : i + 1, :] = jnp.sum(acc[2 + i], axis=0, keepdims=True)
            exchange(early, early_c, 0, core_peer).start()
            return
        landing = early_c if k == 1 else early_r.at[k - 2]
        exchange(early, landing, k - 1, core_peer if k == 1 else dp_peer(k - 2)).wait()
        early[...] = early[...] + landing[...]
        if k == 1:
            early[4:5, :] = jnp.sum(acc[6], axis=0, keepdims=True)
        if k <= levels:
            exchange(early, early_r.at[k - 1], k, dp_peer(k - 1)).start()

    tiles = width // 128

    def late_step(k):
        first = 1 + levels
        if k == 0:
            late[...] = jnp.zeros_like(late)
            for i in range(2):
                row = jnp.sum(acc[i], axis=0, keepdims=True)
                for j in range(tiles):
                    late[i * tiles + j : i * tiles + j + 1, :] = row[:, j * 128 : (j + 1) * 128]
            exchange(late, late_c, first, core_peer).start()
            return
        landing = late_c if k == 1 else late_r.at[k - 2]
        exchange(late, landing, first + k - 1, core_peer if k == 1 else dp_peer(k - 2)).wait()
        late[...] = late[...] + landing[...]
        if k == 1:
            for h in range(heads):
                row = jnp.sum(acch[h], axis=0, keepdims=True)
                late[2 * tiles + h : 2 * tiles + h + 1, 0:HD] = row[:, 0:HD]
                late[2 * tiles + h : 2 * tiles + h + 1, HD : 2 * HD] = row[:, 2 * HD : 3 * HD]
        if k <= levels:
            exchange(late, late_r.at[k - 1], first + k, dp_peer(k - 1)).start()

    def norm_rows(s):
        for half, start in enumerate(half_start):

            def step(off, carry):
                xn, _ = normalize(group_rows(tok, s, start + off, 16))
                normed[slot_rows(s, half * HALF + off, 16), :] = (xn * gain1[...] + shift1[...]).astype(BF)
                return carry

            row_loop(HALF, 16, 6, step, 0)

    def mask_rows(s):
        for half, start in enumerate(half_start):

            def step(off, carry):
                ok = inside(s, lax.broadcasted_iota(jnp.int32, (16, 1), 0) + (start + off))
                value = group_rows(hidden, s, start + off, 16)
                cot[slot_rows(s, half * HALF + off, 16), :] = jnp.where(ok, value, 0.0).astype(BF)
                return carry

            row_loop(HALF, 16, 6, step, 0)

    loads[0].wait()
    norm_rows(0)
    pl.semaphore_wait(bar, len(peers))
    loads[2].wait()
    w_own = [
        remote(wout.at[my_quarter], wout.at[my_quarter], w_send.at[0], w_recv.at[0], core_peer),
        remote(wout.at[my_quarter], wout.at[my_quarter], w_send.at[1], w_recv.at[1], y_peer),
    ]
    w_pass = remote(wout.at[its_quarter], wout.at[its_quarter], w_send.at[2], w_recv.at[2], core_peer)
    for copy in w_own:
        copy.start()
    loads[1].wait()
    norm_rows(1)
    for h in range(heads):
        for j in range(3):
            wstack[h, j * HD : (j + 1) * HD, :] = wqkv[j, h * HD : (h + 1) * HD, :]

    def a_swap(s):
        return remote(att.at[slot_rows(s, other, HALF)], attc.at[s], a_send.at[s, 0], a_recv.at[s, 0], core_peer)

    def a_copy(s):
        return remote(attf.at[s, side], attf.at[s, side], a_send.at[s, 1], a_recv.at[s, 1], y_peer)

    def project(s):
        def half(i, carry):
            r = slot_rows(s, i * HALF, HALF)
            x = normed[r, :]
            qkv[0, r, :] = (dot_nt(x, wqkv[0]) + qvb[0:1, :]).astype(BF)
            qkv[1, r, :] = dot_nt(x, wqkv[1]).astype(BF)
            qkv[2, r, :] = (dot_nt(x, wqkv[2]) + qvb[1:2, :]).astype(BF)
            return carry

        lax.fori_loop(0, 2, half, 0)

    def attend(s):
        whole = slot_rows(s, 0, SLOT)
        key = lax.broadcasted_iota(jnp.int32, (1, SLOT), 1)
        key = key + jnp.where(key < HALF, half_start[0], half_start[1] - HALF)
        key_bias = jnp.where(inside(s, key), 0.0, MASKED)

        def half(i, carry):
            r = slot_rows(s, i * HALF, HALF)
            for h in range(heads):
                lanes = slice(h * HD, (h + 1) * HD)
                q = (qkv[0, r, lanes] * HD**-0.5).astype(BF)
                scores = dot_nt(q, qkv[1, whole, lanes]) + key_bias
                exps = jnp.exp(scores - jnp.max(scores, axis=-1, keepdims=True))
                weights = (exps * (1.0 / jnp.sum(exps, axis=-1, keepdims=True))).astype(BF)
                probs[s * heads + h, pl.ds(pl.multiple_of(i * HALF, 16), HALF), :] = weights
                att[r, lanes] = dot_nn(weights, qkv[2, whole, lanes]).astype(BF)
            return carry

        lax.fori_loop(0, 2, half, 0)
        a_swap(s).start()

    def join(s):
        a_swap(s).wait()
        mine, its = att[slot_rows(s, own, HALF), :], attc[s]
        left = jnp.where(core == 0, mine, its)
        right = jnp.where(core == 0, its, mine)
        attf[s, side] = jnp.concatenate([left, right], axis=1)
        a_copy(s).start()

    project(0)
    attend(0)
    project(1)
    join(0)
    attend(1)
    w_own[1].wait()
    w_pass.start()
    loads[3].wait()
    mask_rows(0)
    join(1)
    mask_rows(1)
    w_own[0].wait()
    w_pass.wait()
    loads[4].wait()
    loads[5].wait()

    def second_norm(s):
        a_copy(s).wait()
        tmp_a[...] = dot_nn(jnp.concatenate([attf[s, 0], attf[s, 1]], axis=1), wout[...])

        def step(off, carry):
            r = pl.ds(off, 16)
            m = tmp_a[r, :] + group_rows(tok, s, half_start[0] + off, 16) + bias_out[...]
            middle[s, r, :] = m
            xn, _ = normalize(m)
            normed2[s][0][r, :] = (xn * gain2[...] + shift2[...]).astype(BF)
            return carry

        row_loop(HALF, 16, 6, step, 0)
        half_copy(normed2, s, 0).start()

    def up_half(s, half):
        tmp_a[...] = dot_nn(normed2[s][half][...], wup[...])

        def step(off, carry):
            g = slot_rows(s, half * HALF + off, 16)
            x = tmp_a[pl.ds(off, 16), :] + bias_up[...]
            phi = 0.5 + 0.5 * lax.erf(x * 0.7071067811865476)
            hidden[g, :] = (x * phi).astype(BF)
            slope[g, :] = phi + x * (jnp.exp(x * x * -0.5) * 0.3989422804014327)
            return carry

        row_loop(HALF, 16, 2, step, 0)

    def back_half(s, half):
        tmp_a[...] = dot_nt(cot[slot_rows(s, half * HALF, HALF), :], wdown[...])

        def step(off, sums):
            g = slot_rows(s, half * HALF + off, 16)
            low = (tmp_a[pl.ds(off, 16), :] * slope[g, :]).astype(BF)
            pregrad[g, :] = low
            return sums + fold8(low.astype(F32))

        acc[6] += row_loop(HALF, 16, 6, step, zero8)

    def unit_grad(u, left, right):
        row0, size, _ = units[u]
        gbuf[row0 : row0 + size, :] = dot_tn(left, right[...]).astype(BF)
        dp_rs(u, 0).start()

    def norm_columns(columns):
        return jnp.concatenate([ref[:, columns] for refs in normed2 for ref in refs], axis=0)

    lower, upper = slice(0, width // 2), slice(width // 2, width)
    def norm_part(s):
        begin(s, 0, lambda off: dot_nt(pregrad[slot_rows(s, off, HALF), :], wup[...]))

    def out_part(s):
        begin(s, 1, lambda off: dot_nn(hidden[slot_rows(s, off, HALF), :], wdown[...]))

    second_norm(0)
    up_half(0, 0)
    half_copy(normed2, 0, 0).wait()
    up_half(0, 1)
    back_half(0, 1)
    back_half(0, 0)
    norm_part(0)
    second_norm(1)
    end(0, 0)
    up_half(1, 0)
    half_copy(normed2, 1, 0).wait()
    up_half(1, 1)
    unit_grad(0, hidden[:, lower], cot)
    unit_grad(1, hidden[:, upper], cot)
    back_half(1, 1)
    back_half(1, 0)
    norm_part(1)
    unit_grad(2, norm_columns(lower), pregrad)
    end(1, 0)
    out_part(0)
    unit_grad(3, norm_columns(upper), pregrad)
    end(0, 1)
    out_part(1)

    def second_back(s):
        y_copy(s, 0).wait()

        def step(off, sums):
            r = pl.ds(off, 16)
            g = slot_rows(s, own + off, 16)
            n = total(s, 0, r)
            xn, scale = normalize(middle[s, r, :])
            og = cot[g, :].astype(F32)
            m = og + norm_back(n * gain2[...], xn, scale)
            midgrad[s, r, :] = m
            mg[s][0][r, :] = m.astype(BF)
            return tuple(a + fold8(b) for a, b in zip(sums, (n * xn, n, m, og), strict=True))

        sums = row_loop(HALF, 16, 3, step, (zero8,) * 4)
        for i in range(4):
            acc[2 + i] += sums[i]
        half_copy(mg, s, 1).start()

    def head_back(s, h):
        whole = slot_rows(s, 0, SLOT)
        lanes = slice(h * HD, (h + 1) * HD)
        keys, values = qkv[1, whole, lanes], qkv[2, whole, lanes]
        for c in (0, 1):
            r = slot_rows(s, c * HALF, HALF)
            part = slice(c * HALF, (c + 1) * HALF)
            p = probs[s * heads + h, part, :].astype(F32)
            prob_grad = dot_nt(agrad[r, lanes], values)
            inner = jnp.sum(p * prob_grad, axis=-1, keepdims=True)
            sgrad[part, :] = (p * (prob_grad - inner)).astype(BF)
            dhead[h, r, 0:HD] = (dot_nn(sgrad[part, :], keys) * HD**-0.5).astype(BF)
            serve(f"head{s}{h}{c}")
        dhead[h, whole, HD : 2 * HD] = (dot_tn(sgrad[...], qkv[0, whole, lanes]) * HD**-0.5).astype(BF)
        dhead[h, whole, 2 * HD : 3 * HD] = dot_tn(probs[s * heads + h], agrad[whole, lanes]).astype(BF)
        acch[h] += fold8(dhead[h, whole, :].astype(F32))

    def attended_grad(s):
        half_copy(mg, s, 1).wait()
        agrad[slot_rows(s, 0, SLOT), :] = dot_nt(
            jnp.concatenate([mg[s][0][...], mg[s][1][...]], axis=0), wout[my_quarter, :]
        ).astype(BF)

    def projected(s):
        def part(off):
            r = slot_rows(s, off, HALF)
            return sum(dot_nn(dhead[h, r, :], wstack[h]) for h in range(heads))

        begin(s, 2, part)

    second_back(0)
    end(1, 1)
    serve("back0")
    attended_grad(0)
    for h in range(heads - 1):
        head_back(0, h)
    second_back(1)
    serve("back1")
    head_back(0, heads - 1)
    projected(0)
    attended_grad(1)
    end(0, 2)
    all_mg = jnp.concatenate([ref[...] for refs in mg for ref in refs], axis=0)
    gbuf[2 * width : 2 * width + third, :] = dot_tn(att[...], all_mg).astype(BF)
    dp_rs(4, 0).start()
    serve("out")
    for h in range(heads):
        head_back(1, h)
        if h == heads - 1:
            projected(1)
        unit_grad(5 + h, dhead[h], normed)
    serve("heads")
    end(1, 2)

    def finish_block(s):
        y_copy(s, 1).wait()

        def step(off, carry):
            r = pl.ds(off, 16)
            block[slot_rows(s, half_start[0] + off, 16), :] = (middle[s, r, :] + total(s, 1, r) + bias_down[...]).astype(BF)
            return carry

        row_loop(HALF, 16, 6, step, 0)
        gather_copy(block, s, 2).start()

    def finish_grad(s):
        y_copy(s, 2).wait()

        def step(off, sums):
            r = pl.ds(off, 16)
            n = total(s, 2, r)
            xn, scale = normalize(group_rows(tok, s, half_start[0] + off, 16))
            ingrad[slot_rows(s, half_start[0] + off, 16), :] = (midgrad[s, r, :] + norm_back(n * gain1[...], xn, scale)).astype(BF)
            return tuple(a + fold8(b) for a, b in zip(sums, (n * xn, n), strict=True))

        sums = row_loop(HALF, 16, 4, step, (zero8,) * 2)
        for i in range(2):
            acc[i] += sums[i]
        gather_copy(ingrad, s, 3).start()

    def assemble(ref):
        def step(off, carry):
            index = lax.broadcasted_iota(jnp.int32, (16, 1), 0) + off

            def two_from(start):
                source = jnp.clip(off - start, 0, SLOT - 16) + SLOT
                return ref[pl.ds(pl.multiple_of(source, 16), 16), :].astype(F32)

            two = jnp.where(first_small, two_from(SMALL_START), two_from(LARGE_START))
            low = jnp.minimum(off, SLOT - 16)
            one = ref[pl.ds(pl.multiple_of(low, 16), 16), :].astype(F32)
            both = jnp.where(index < first_len, one, two)
            ref[pl.ds(off, 16), :] = jnp.where(index < first_len + second_len, both, 0.0).astype(BF)
            return carry

        row_loop(rows, 16, 1, step, 0)

    finish_block(0)
    finish_block(1)
    for s in (0, 1):
        gather_copy(block, s, 2).wait()
    assemble(block)
    out_block = local(14, block.at[0:rows], block_h)
    out_block.start()
    serve("block")
    finish_grad(0)
    serve("grad0")
    finish_grad(1)
    late_step(0)
    for s in (0, 1):
        gather_copy(ingrad, s, 3).wait()
    assemble(ingrad)
    out_grad = local(15, ingrad.at[0:rows], ingrad_h)
    out_grad.start()
    serve("grad1")
    for k in range(5, levels + 2):
        early_step(k)
        late_step(k)

    small_o[...] = jnp.zeros_like(small_o)
    for i in range(2):
        for j in range(tiles):
            small_o[i : i + 1, j * 128 : (j + 1) * 128] = late[i * tiles + j : i * tiles + j + 1, :]
    small_o[2:6, :] = early[0:4, :]
    small_o[8:9, :] = early[4:5, :]
    for h in range(heads):
        row = late[2 * tiles + h : 2 * tiles + h + 1, :]
        small_o[9:10, h * HD : (h + 1) * HD] = row[:, 0:HD]
        small_o[10:11, h * HD : (h + 1) * HD] = row[:, HD : 2 * HD]
    out_block.wait()
    out_grad.wait()
    for u in range(len(units)):
        dp_out(u).wait()


def unpack_kernel(block, ingrad, down, up, out, qkv0, qkv1, qkv2, small, *outs):
    outs[0][...] = block[...]
    outs[1][...] = ingrad[...].astype(F32)
    outs[2][...] = down[...].astype(F32)
    outs[3][...] = up[...].astype(F32)
    outs[4][...] = out[...].astype(F32)
    for i, qkv in enumerate((qkv0, qkv1, qkv2)):
        rows = qkv.shape[0]
        outs[5][i * rows : (i + 1) * rows, :] = qkv[...].astype(F32)

    @pl.when(pl.program_id(0) == 0)
    def _():
        for i, row in enumerate((0, 1, 2, 3, 4, 5, 8)):
            outs[6 + i][...] = small[row]
        outs[13][...] = small[9:11, 0 : outs[13].shape[1]]


def call_unpack(block, ingrad, grads, small, third):
    rows, width = block.shape
    steps = 6
    row_block = -(-rows // (16 * steps)) * 16

    def part(size, start):
        return pl.BlockSpec((size, width), lambda i: (start // size + i, 0))

    def whole(shape):
        return pl.BlockSpec(shape, lambda i: (0,) * len(shape))

    big, mid, low = width // steps, 3 * third // steps, third // steps
    piece = mid // 3
    per_head = HD // piece

    def qkv_part(b, i):
        m = 3 * i + b
        kind, rest = m // (third // piece), m % (third // piece)
        head, low_part = rest // per_head, rest % per_head
        return (2 * width + third) // piece + (head * 3 + kind) * per_head + low_part, 0

    shapes = [
        ((rows, width), BF, part(row_block, 0)),
        ((rows, width), F32, part(row_block, 0)),
        ((width, width), F32, part(big, 0)),
        ((width, width), F32, part(big, 0)),
        ((third, width), F32, part(low, 0)),
        ((3 * third, width), F32, part(mid, 0)),
    ]
    shapes += [((width,), F32, whole((width,)))] * 7 + [((2, third), F32, whole((2, third)))]
    return pl.pallas_call(
        unpack_kernel,
        grid=(steps,),
        out_shape=[jax.ShapeDtypeStruct(shape, kind) for shape, kind, _ in shapes],
        in_specs=[
            part(row_block, 0),
            part(row_block, 0),
            part(big, 0),
            part(big, width),
            part(low, 2 * width),
            *(pl.BlockSpec((piece, width), functools.partial(qkv_part, b)) for b in range(3)),
            whole(small.shape),
        ],
        out_specs=[spec for _, _, spec in shapes],
    )(block, ingrad, grads, grads, grads, grads, grads, grads, small)


def call_layer(n_dp, *operands):
    rows, width = operands[2].shape
    third = operands[5].shape[0]
    heads = third // HD
    levels = n_dp.bit_length() - 1
    extra = max(levels - 3, 1)
    slots = 2 * SLOT
    grad_rows = 2 * width + 4 * third
    vmem = pl.BlockSpec(memory_space=pltpu.VMEM)
    smem = pl.BlockSpec(memory_space=pltpu.SMEM)
    hbm = pl.BlockSpec(memory_space=pl.ANY)
    dma = pltpu.SemaphoreType.DMA
    return pl.pallas_call(
        functools.partial(layer_kernel, n_dp),
        out_shape=(
            jax.ShapeDtypeStruct((rows, width), BF),
            jax.ShapeDtypeStruct((rows, width), BF),
            jax.ShapeDtypeStruct((grad_rows, width), BF),
            jax.ShapeDtypeStruct((16, width), F32),
        ),
        in_specs=[smem] * 2 + [hbm] * 6 + [vmem] * 8,
        out_specs=(hbm, hbm, hbm, vmem),
        scratch_shapes=[
            pltpu.VMEM((rows + 16, width), BF),
            pltpu.VMEM((slots, width), BF),
            pltpu.VMEM((3, third, width), BF),
            pltpu.VMEM((4 * third, width), BF),
            pltpu.VMEM((width, width), BF),
            pltpu.VMEM((width, width), BF),
            pltpu.VMEM((8, width), F32),
            pltpu.VMEM((slots, width), BF),
            pltpu.VMEM((3, slots, third), BF),
            pltpu.VMEM((slots, third), BF),
            pltpu.VMEM((2, HALF, third), BF),
            pltpu.VMEM((2, 2, HALF, 2 * third), BF),
            pltpu.VMEM((2 * heads, SLOT, SLOT), BF),
            pltpu.VMEM((slots, width), BF),
            pltpu.VMEM((slots, width), BF),
            pltpu.VMEM((2, HALF, width), F32),
            pltpu.VMEM((2, HALF, width), F32),
            pltpu.VMEM((HALF, width), F32),
            pltpu.VMEM((slots, third), BF),
            pltpu.VMEM((heads, slots, third), BF),
            pltpu.VMEM((heads, third, width), BF),
            pltpu.VMEM((SLOT, SLOT), BF),
            pltpu.VMEM((slots, width), F32),
            pltpu.VMEM((HALF, width), F32),
            pltpu.VMEM((7, 8, width), F32),
            pltpu.VMEM((heads, 8, third), F32),
            pltpu.VMEM((HALF, width), BF),
            pltpu.VMEM((2, 3, HALF, width), BF),
            pltpu.VMEM((2, 3, HALF, width), BF),
            pltpu.VMEM((2, 3, HALF, width), BF),
            pltpu.VMEM((grad_rows, width), BF),
            pltpu.VMEM((grad_rows, width), BF),
            pltpu.VMEM((width // 8 if levels > 3 else 16, width), BF),
            pltpu.VMEM((8, width), F32),
            pltpu.VMEM((16, 128), F32),
            pltpu.VMEM((slots, width), BF),
            pltpu.VMEM((slots, width), BF),
            pltpu.VMEM((8, width), F32),
            pltpu.VMEM((levels, 8, width), F32),
            pltpu.VMEM((16, 128), F32),
            pltpu.VMEM((levels, 16, 128), F32),
            dma((16,)),
            dma((3,)),
            dma((3,)),
            dma((2, 2)),
            dma((2, 2)),
            dma((2, 3)),
            dma((2, 3)),
            dma((2, 3)),
            dma((2, 3)),
            dma((2, 4)),
            dma((2, 4)),
            dma((8, 5 + extra)),
            dma((8, 5 + extra)),
            dma((2 + 2 * levels,)),
            dma((2 + 2 * levels,)),
            pltpu.SemaphoreType.REGULAR((extra,)),
        ]
        + [pltpu.VMEM((size >> min(i + 1, 2), width), BF) for _, size, _ in dp_units(width, third) for i in range(3)]
        + [pltpu.VMEM((HALF, width), BF)] * 8,
        compiler_params=pltpu.CompilerParams(
            collective_id=0, has_side_effects=True, vmem_limit_bytes=67043328
        ),
    )(*operands)


def body(
    n_dp,
    tokens,
    cotangent,
    image_group,
    image_length,
    first_gain,
    first_shift,
    qkv_weight,
    qv_bias,
    out_weight,
    out_bias,
    second_gain,
    second_shift,
    up_weight,
    up_bias,
    down_weight,
    down_bias,
):
    third = out_weight.shape[0]
    width = tokens.shape[1]
    block, ingrad, grads, small = call_layer(
        n_dp,
        image_group,
        image_length,
        tokens,
        cotangent,
        jnp.transpose(qkv_weight, (1, 2, 0)),
        out_weight,
        up_weight,
        down_weight,
        first_gain,
        first_shift,
        out_bias,
        second_gain,
        second_shift,
        down_bias,
        up_bias,
        qv_bias,
    )
    outs = call_unpack(block, ingrad, grads, small, third)
    block_out, input_grad, down_grad, up_grad, out_grad, qkv_grad = outs[:6]
    g1, b1, g2, b2, out_bias_grad, down_bias_grad, up_bias_grad, qv_bias_grad = outs[6:]
    return (
        block_out,
        input_grad,
        g1,
        b1,
        jnp.transpose(qkv_grad.reshape(3, third, width), (2, 0, 1)),
        qv_bias_grad,
        out_grad,
        out_bias_grad,
        g2,
        b2,
        up_grad,
        up_bias_grad,
        down_grad,
        down_bias_grad,
    )


def solution(mesh):
    in_specs = (
        P("dp", None),
        P("dp", None),
        P(),
        P(),
        P(),
        P(),
        P(None, None, "tensor"),
        P(None, "tensor"),
        P("tensor", None),
        P(),
        P(),
        P(),
        P(None, "tensor"),
        P("tensor"),
        P("tensor", None),
        P(),
    )
    out_specs = (
        P("dp", None),
        P("dp", None),
        P(),
        P(),
        P(None, None, "tensor"),
        P(None, "tensor"),
        P("tensor", None),
        P(),
        P(),
        P(),
        P(None, "tensor"),
        P("tensor"),
        P("tensor", None),
        P(),
    )
    return jax.shard_map(
        functools.partial(body, mesh.shape["dp"]), mesh=mesh, in_specs=in_specs, out_specs=out_specs, check_vma=False
    )
```
